256 devices in a mesh: section: 8 (over y_hi, x), dp: 32 (over z, y_lo, core).
Axes of the slice: x: 4, y: 4 (y_hi: 2, y_lo: 2; y = y_hi * 2 + y_lo), z: 8, core: 2. Of those that a mesh axis runs over, the one named last changes fastest.
Arguments:
- tokens: bfloat16 [15360, 2048], P('dp'), may hold values from -6 to 6
- cotangent: bfloat16 [15360, 2048], P('dp'), may hold values from -6 to 6
- w_gate: bfloat16 [8, 2048, 512], P('section'), may hold values from -0.125 to 0.125
- w_up: bfloat16 [8, 2048, 512], P('section'), may hold values from -0.125 to 0.125
- w_down: bfloat16 [8, 2048, 512], P('section'), may hold values from -0.25 to 0.25
Outputs:
- input_grad: bfloat16 [8, 15360, 2048], P('section', 'dp')
- grad_gate: float32 [8, 2048, 512], P('section', 'dp')
- grad_up: float32 [8, 2048, 512], P('section', 'dp')
- grad_down: float32 [8, 2048, 512], P('section', 'dp')
The draws below stay inside these ranges and needn't reach their ends.
All inputs are finite; a program needn't handle non-finite values.
Results may differ from the reference program's by a relative error of at most 0.035.
Values may be sent and summed in bfloat16 or wider, within the bound.
A program may use at most 128 MiB of HBM per device.

```python
import jax
import jax.numpy as jnp
from jax import lax

D = 2048
F = 512
TOKENS = 15360
LAYERS = 8


def spiked(result, stream_key, source, target, blocks, factor):
    def block_of(axis_at):
        return (jnp.arange(result.shape[axis_at]) // (result.shape[axis_at] // blocks)).reshape((-1,) + (1,) * (result.ndim - 1 - axis_at))

    one_side = jax.random.permutation(stream_key, blocks)[block_of(target)]
    far = (block_of(target) + blocks // 2) % blocks
    return jnp.where((block_of(source) == one_side) | (block_of(source) == far), factor * result, result)


def level_of(stream_key, shape, shards, smallest, largest):
    level, own = 1.0, jax.random.fold_in(stream_key, 6)
    for dim, blocks in shards:
        heights = jnp.exp(jax.random.uniform(jax.random.fold_in(own, dim), (blocks,), jnp.float32, smallest / len(shards), largest / len(shards)))
        level = level * jnp.repeat(heights, shape[dim] // blocks).reshape([-1 if axis == dim else 1 for axis in range(len(shape))])
    return level


def normal_values(stream_key, shape, width, bound, shards=(), kind=jnp.bfloat16):
    values = jax.random.normal(stream_key, shape, jnp.float32) * width
    if len(shards) > 0:
        values = level_of(stream_key, shape, shards, -0.22, 0.18) * values
    return jnp.clip(values, min=-bound, max=bound).astype(kind)


def heavy_noise(own_key, shape, width, reach, pieces, heavy, kind=jnp.bfloat16):
    values = width * jax.random.normal(own_key, shape, jnp.float32)
    if pieces:
        values = values * level_of(own_key, shape, pieces, -0.22, 0.18)
    return jnp.clip(spiked(values, jax.random.fold_in(own_key, 3), *heavy), -reach, reach).astype(kind)


def setup_inputs(seed: int = 0) -> dict:
    streams_of = jax.random.split(jax.random.key(seed), 6)
    return {
        "tokens": heavy_noise(streams_of[0], (TOKENS, D), 1.0, 6.0, ((0, 32),), (0, 1, 32, 2.75)),
        "cotangent": heavy_noise(streams_of[1], (TOKENS, D), 1.0, 6.0, ((0, 32),), (0, 1, 32, 2.75)),
        "w_gate": normal_values(streams_of[2], (LAYERS, D, F), D ** -0.5, 0.125, ((0, 8),)),
        "w_up": normal_values(streams_of[3], (LAYERS, D, F), D ** -0.5, 0.125, ((0, 8),)),
        "w_down": normal_values(streams_of[4], (LAYERS, D, F), F ** -0.5, 0.25, ((0, 8),)),
    }


def forward_layer(layer_input_rows, w_gate, w_up, w_down):
    xf = layer_input_rows.astype(jnp.float32)
    inverse_norm_scale = lax.rsqrt(lax.optimization_barrier(jnp.mean(xf * xf, axis=-1, keepdims=True)) + 1e-06)
    normed = (xf * inverse_norm_scale).astype(jnp.bfloat16)
    gate = jnp.dot(normed, w_gate, preferred_element_type=jnp.float32)
    upper = jnp.dot(normed, w_up, preferred_element_type=jnp.float32)
    hidden = (gate * jax.nn.sigmoid(gate) * upper).astype(jnp.bfloat16)
    branch = lax.dot_general(hidden, w_down, (((1,), (1,)), ((), ())), preferred_element_type=jnp.float32)
    return ((xf + branch).astype(jnp.bfloat16), normed, inverse_norm_scale, gate, upper, hidden)

def backward_layer(layer_input_rows, arriving_gradient, inverse_norm_scale, gate, upper, w_gate, w_up, w_down):
    d_hidden = jnp.dot(arriving_gradient, w_down, preferred_element_type=jnp.float32)
    sig = jax.nn.sigmoid(gate)
    d_gate = (d_hidden * upper * sig * (1.0 + gate * (1.0 - sig))).astype(jnp.bfloat16)
    d_upper = (d_hidden * gate * sig).astype(jnp.bfloat16)
    dims = (((1,), (1,)), ((), ()))
    normalized_gradient = lax.dot_general(d_gate, w_gate, dims, preferred_element_type=jnp.float32)
    normalized_gradient = normalized_gradient + lax.dot_general(d_upper, w_up, dims, preferred_element_type=jnp.float32)
    normalized_input = layer_input_rows.astype(jnp.float32) * inverse_norm_scale
    inner_product_sum = lax.optimization_barrier(jnp.mean(normalized_gradient * normalized_input, axis=-1, keepdims=True))
    input_gradient_rows = (arriving_gradient.astype(jnp.float32) + inverse_norm_scale * (normalized_gradient - normalized_input * inner_product_sum)).astype(jnp.bfloat16)
    return (input_gradient_rows, d_gate, d_upper)

def reference(tokens, cotangent, w_gate, w_up, w_down):
    rows_dims = (((0,), (0,)), ((), ()))
    current = tokens
    inputs = []
    for layer in range(LAYERS):
        inputs.append(current)
        current = forward_layer(current, w_gate[layer], w_up[layer], w_down[layer])[0]
    arriving_gradient = cotangent
    grads_in = [None] * LAYERS
    grads_g = [None] * LAYERS
    grads_u = [None] * LAYERS
    grads_d = [None] * LAYERS
    for layer in reversed(range(LAYERS)):
        layer_input_rows = inputs[layer]
        _, normed, inverse_norm_scale, gate, upper, hidden = forward_layer(layer_input_rows, w_gate[layer], w_up[layer], w_down[layer])
        input_gradient_rows, d_gate, d_upper = backward_layer(layer_input_rows, arriving_gradient, inverse_norm_scale, gate, upper, w_gate[layer], w_up[layer], w_down[layer])
        grads_g[layer] = lax.dot_general(normed, d_gate, rows_dims, preferred_element_type=jnp.float32)
        grads_u[layer] = lax.dot_general(normed, d_upper, rows_dims, preferred_element_type=jnp.float32)
        grads_d[layer] = lax.dot_general(arriving_gradient, hidden, rows_dims, preferred_element_type=jnp.float32)
        grads_in[layer] = input_gradient_rows
        arriving_gradient = input_gradient_rows
    return (jnp.stack(grads_in), jnp.stack(grads_g), jnp.stack(grads_u), jnp.stack(grads_d))
```

```python
import functools

import jax
import jax.numpy as jnp
from jax import lax
from jax.experimental import pallas as pl
from jax.experimental.pallas import tpu as pltpu
from jax.sharding import Mesh
from jax.sharding import PartitionSpec as P

MICRO = 15
AHEAD = 3
CHUNKS = 2
DP = ("dp_0", "dp_1", "dp_2")
MESH = pl.DeviceIdType.MESH
F32 = jnp.float32
BF16 = jnp.bfloat16
ROWS_ROWS = (((0,), (0,)), ((), ()))
LAST_LAST = (((1,), (1,)), ((), ()))


def reduced_to_own(blocks, axes, sequence):
    inside = blocks.shape[1:]
    blocks = blocks.reshape(*(lax.axis_size(a) for a in axes), *inside)
    blocks = jnp.moveaxis(blocks, sequence, range(len(axes))).reshape(-1, *inside)
    for k in sequence:
        blocks = lax.psum_scatter(blocks, axes[k], scatter_dimension=0, tiled=True)
    return blocks[0]


def pipeline_kernel(
    sections,
    micro,
    tok,
    cot,
    wg_h,
    wu_h,
    wd_h,
    grad_in,
    part,
    wg,
    wu,
    wd,
    x_in,
    g_in,
    x_out,
    g_out,
    gate_s,
    up_s,
    hid_s,
    dg_s,
    du_s,
    r_s,
    part_v,
    w_sem,
    x_recv,
    g_recv,
    x_send,
    g_send,
    c_send,
    o_send,
    o_recv,
    p_sem,
):
    place = lax.axis_index("section")
    side = lax.axis_index("dp_1")
    half = sections // 2
    last = sections - 1
    upper = place >= half
    width = x_in.shape[2]
    units = wg.shape[1]
    span = width // CHUNKS

    weights = [
        pltpu.make_async_copy(src, dst, w_sem.at[k])
        for k, (src, dst) in enumerate(((wg_h, wg), (wu_h, wu), (wd_h, wd)))
    ]
    for copy in weights:
        copy.start()

    @pl.when(place == 0)
    def _():
        @pl.loop(0, micro)
        def _(m):
            pltpu.make_async_copy(tok.at[m], x_in.at[m], x_recv.at[m]).start()

    next_side = jnp.where(place == half - 1, 1 - side, side)
    prev_side = jnp.where(place == half, 1 - side, side)
    after = {"section": lax.rem(place + 1, sections), "dp_1": next_side}
    before = {"section": lax.rem(place + sections - 1, sections), "dp_1": prev_side}
    partner = {"dp_1": 1 - side}

    barrier = pltpu.get_barrier_semaphore()

    @pl.when(place < last)
    def _():
        pl.semaphore_signal(barrier, inc=1, device_id=after, device_id_type=MESH)

    @pl.when(place > 0)
    def _():
        pl.semaphore_signal(barrier, inc=1, device_id=before, device_id_type=MESH)

    @pl.when(upper)
    def _():
        pl.semaphore_signal(barrier, inc=1, device_id=partner, device_id_type=MESH)

    expected = (
        jnp.where(place < last, 1, 0) + jnp.where(place > 0, 1, 0) + jnp.where(upper, 1, 0)
    )
    pl.semaphore_wait(barrier, expected)

    @pl.when(place == last)
    def _():
        @pl.loop(0, micro)
        def _(m):
            pltpu.make_async_remote_copy(
                cot.at[m], g_in.at[m], c_send, g_recv.at[m], device_id=partner, device_id_type=MESH
            ).start()

    for copy in weights:
        copy.wait()

    def forward(m):
        pltpu.make_async_copy(x_in.at[m], x_in.at[m], x_recv.at[m]).wait()
        x = x_in[m]
        gate = jnp.dot(x, wg[...], preferred_element_type=F32)
        up = jnp.dot(x, wu[...], preferred_element_type=F32)
        xf = x.astype(F32)
        r = lax.rsqrt(jnp.mean(xf * xf, axis=-1, keepdims=True) + 1e-06)
        gate = gate * r
        up = up * r
        hidden = (gate * jax.nn.sigmoid(gate) * up).astype(BF16)
        gate_s[m] = gate
        up_s[m] = up
        hid_s[m] = hidden
        r_s[m] = jnp.broadcast_to(r, (r.shape[0], 128))

        @pl.when(place < last)
        def _():
            for k in range(CHUNKS):
                cols = slice(k * span, (k + 1) * span)
                branch = lax.dot_general(
                    hidden, wd[cols, :], LAST_LAST, preferred_element_type=F32
                )
                x_out[m, :, cols] = (x_in[m, :, cols].astype(F32) + branch).astype(BF16)
                pltpu.make_async_remote_copy(
                    x_out.at[m, :, cols],
                    x_in.at[m, :, cols],
                    x_send,
                    x_recv.at[m],
                    device_id=after,
                    device_id_type=MESH,
                ).start()

    def backward(m):
        pltpu.make_async_copy(g_in.at[m], g_in.at[m], g_recv.at[m]).wait()
        d_hidden = jnp.dot(g_in[m], wd[...], preferred_element_type=F32)
        gate = gate_s[m]
        up = up_s[m]
        r = r_s[m, :, 0:1]
        sig = jax.nn.sigmoid(gate)
        d_gate = d_hidden * up * sig * (1.0 + gate * (1.0 - sig))
        d_up = d_hidden * gate * sig
        dg = d_gate.astype(BF16)
        du = d_up.astype(BF16)
        inner = jnp.sum(
            dg.astype(F32) * gate + du.astype(F32) * up, axis=-1, keepdims=True
        ) * (1.0 / width)
        shrink = r * inner
        for k in range(CHUNKS):
            cols = slice(k * span, (k + 1) * span)
            normed_grad = lax.dot_general(dg, wg[cols, :], LAST_LAST, preferred_element_type=F32)
            normed_grad = normed_grad + lax.dot_general(
                du, wu[cols, :], LAST_LAST, preferred_element_type=F32
            )
            g_out[m, :, cols] = (
                g_in[m, :, cols].astype(F32)
                + r * (normed_grad - x_in[m, :, cols].astype(F32) * shrink)
            ).astype(BF16)

            @pl.when(place > 0)
            def _():
                pltpu.make_async_remote_copy(
                    g_out.at[m, :, cols],
                    g_in.at[m, :, cols],
                    g_send,
                    g_recv.at[m],
                    device_id=before,
                    device_id_type=MESH,
                ).start()

        @pl.when(upper)
        def _():
            pltpu.make_async_remote_copy(
                g_out.at[m],
                grad_in.at[m],
                o_send,
                o_recv,
                device_id=partner,
                device_id_type=MESH,
            ).start()

        @pl.when(jnp.logical_not(upper))
        def _():
            pltpu.make_async_copy(g_out.at[m], grad_in.at[m], o_recv).start()

        dg_s[m] = (d_gate * r).astype(BF16)
        du_s[m] = (d_up * r).astype(BF16)

    lead = jnp.minimum(1 + AHEAD * (last - place), micro)

    @pl.loop(0, micro + lead)
    def _(i):
        @pl.when(i >= lead)
        def _():
            backward(i - lead)

        @pl.when(i < micro)
        def _():
            forward(i)

    rows = micro * x_in.shape[1]
    tile = 256
    dg_all = dg_s[...].reshape(rows, units)
    du_all = du_s[...].reshape(rows, units)
    hid_all = hid_s[...].reshape(rows, units)

    @pl.loop(0, width // tile)
    def _(k):
        at = pl.multiple_of(k * tile, tile)
        xs = x_in[:, :, pl.ds(at, tile)].reshape(rows, tile)
        gs = g_in[:, :, pl.ds(at, tile)].reshape(rows, tile)
        for j, (left, right) in enumerate(((xs, dg_all), (xs, du_all), (gs, hid_all))):
            part_v[pl.ds(at, tile), j * units : (j + 1) * units] = lax.dot_general(
                left, right, ROWS_ROWS, preferred_element_type=F32
            ).astype(BF16)
        pltpu.make_async_copy(
            part_v.at[pl.ds(at, tile)], part.at[pl.ds(at, tile)], p_sem
        ).start()

    pltpu.make_async_copy(part_v, part, p_sem).wait()

    @pl.when(place < last)
    def _():
        pltpu.make_async_copy(x_out, x_out, x_send).wait()

    @pl.when(place > 0)
    def _():
        pltpu.make_async_copy(g_out, g_out, g_send).wait()

    @pl.when(place == last)
    def _():
        pltpu.make_async_copy(g_in, g_in, c_send).wait()

    @pl.when(upper)
    def _():
        pltpu.make_async_copy(g_out, g_out, o_send).wait()

    pltpu.make_async_copy(g_out, grad_in, o_recv).wait()


def run_pipeline(tokens, cotangent, w_gate, w_up, w_down):
    sections = lax.axis_size("section")
    tok_rows, width = tokens.shape
    units = w_gate.shape[1]
    micro = MICRO
    rows = tok_rows // micro
    anywhere = pl.BlockSpec(memory_space=pl.ANY)
    wide = pltpu.VMEM((micro, rows, width), BF16)
    slim = pltpu.VMEM((micro, rows, units), BF16)
    slim_f = pltpu.VMEM((micro, rows, units), F32)
    weight = pltpu.VMEM((width, units), BF16)
    dma = pltpu.SemaphoreType.DMA
    grad_in, part = pl.pallas_call(
        functools.partial(pipeline_kernel, sections, micro),
        out_shape=(
            jax.ShapeDtypeStruct((micro, rows, width), BF16),
            jax.ShapeDtypeStruct((width, 3 * units), BF16),
        ),
        in_specs=[anywhere] * 5,
        out_specs=(anywhere, anywhere),
        scratch_shapes=[
            weight,
            weight,
            weight,
            wide,
            wide,
            wide,
            wide,
            slim_f,
            slim_f,
            slim,
            slim,
            slim,
            pltpu.VMEM((micro, rows, 128), F32),
            pltpu.VMEM((width, 3 * units), BF16),
            dma((3,)),
            dma((micro,)),
            dma((micro,)),
            dma,
            dma,
            dma,
            dma,
            dma,
            dma,
        ],
        compiler_params=pltpu.CompilerParams(
            collective_id=0, has_side_effects=True, vmem_limit_bytes=56 * 1024 * 1024
        ),
        name="pipeline",
    )(
        tokens.reshape(micro, rows, width),
        cotangent.reshape(micro, rows, width),
        w_gate,
        w_up,
        w_down,
    )
    return grad_in.reshape(tok_rows, width), part


def body(tokens, cotangent, w_gate, w_up, w_down):
    units = w_gate.shape[2]
    grad_in, part = run_pipeline(tokens, cotangent, w_gate[0], w_up[0], w_down[0])
    blocks = part.reshape(lax.axis_size(DP), -1, 3 * units)
    summed = reduced_to_own(blocks, DP, (2, 0, 1)).astype(F32)
    grad_g = summed[:, :units]
    grad_u = summed[:, units : 2 * units]
    grad_d = summed[:, 2 * units :]
    return (grad_in[None], grad_g[None], grad_u[None], grad_d[None])


def solution(mesh):
    torus = Mesh(
        mesh.devices.reshape(mesh.shape["section"], 8, 2, 2), ("section", "dp_0", "dp_1", "dp_2")
    )
    placed = (
        P(DP, None),
        P(DP, None),
        P("section", None, None),
        P("section", None, None),
        P("section", None, None),
    )
    return jax.shard_map(
        body,
        mesh=torus,
        in_specs=placed,
        out_specs=(
            P("section", DP, None),
            P("section", DP, None),
            P("section", DP, None),
            P("section", DP, None),
        ),
        check_vma=False,
    )
```

```python
import functools

import jax
import jax.numpy as jnp
from jax import lax
from jax.experimental import pallas as pl
from jax.experimental.pallas import tpu as pltpu
from jax.sharding import Mesh
from jax.sharding import PartitionSpec as P

MICRO = 15
AHEAD = 3
CHUNKS = 2
STREAMS = 4
DP = ("dp_0", "dp_1", "dp_2")
MESH = pl.DeviceIdType.MESH
F32 = jnp.float32
BF16 = jnp.bfloat16
ROWS_ROWS = (((0,), (0,)), ((), ()))
LAST_LAST = (((1,), (1,)), ((), ()))


def pipeline_kernel(
    sections,
    micro,
    tok,
    cot,
    wg_h,
    wu_h,
    wd_h,
    grad_in,
    grad_g,
    grad_u,
    grad_d,
    wg,
    wu,
    wd,
    x_in,
    g_in,
    x_out,
    g_out,
    gate_s,
    up_s,
    hid_s,
    dg_s,
    du_s,
    r_s,
    part,
    from_core,
    ring_in,
    ring_out,
    side_out,
    side_in,
    w_sem,
    x_recv,
    g_recv,
    x_send,
    g_send,
    c_send,
    o_send,
    o_recv,
    core_send,
    core_recv,
    ring_send,
    ring_recv,
    side_send,
    side_recv,
):
    place = lax.axis_index("section")
    deep = lax.axis_index("dp_0")
    side = lax.axis_index("dp_1")
    core = lax.axis_index("dp_2")
    depth = part.shape[0]
    half = sections // 2
    last = sections - 1
    upper = place >= half
    width = x_in.shape[2]
    units = wg.shape[1]
    span = width // CHUNKS

    weights = [
        pltpu.make_async_copy(src, dst, w_sem.at[k])
        for k, (src, dst) in enumerate(((wg_h, wg), (wu_h, wu), (wd_h, wd)))
    ]
    for copy in weights:
        copy.start()

    @pl.when(place == 0)
    def _():
        @pl.loop(0, micro)
        def _(m):
            pltpu.make_async_copy(tok.at[m], x_in.at[m], x_recv.at[m]).start()

    next_side = jnp.where(place == half - 1, 1 - side, side)
    prev_side = jnp.where(place == half, 1 - side, side)
    after = {"section": lax.rem(place + 1, sections), "dp_1": next_side}
    before = {"section": lax.rem(place + sections - 1, sections), "dp_1": prev_side}
    partner = {"dp_1": 1 - side}
    sibling = {"dp_2": 1 - core}
    ring_to = ({"dp_0": lax.rem(deep + 1, depth)}, {"dp_0": lax.rem(deep + depth - 1, depth)})

    barrier = pltpu.get_barrier_semaphore()

    @pl.when(place < last)
    def _():
        pl.semaphore_signal(barrier, inc=1, device_id=after, device_id_type=MESH)

    @pl.when(place > 0)
    def _():
        pl.semaphore_signal(barrier, inc=1, device_id=before, device_id_type=MESH)

    for friend in (partner, sibling, *ring_to):
        pl.semaphore_signal(barrier, inc=1, device_id=friend, device_id_type=MESH)
    expected = 4 + jnp.where(place < last, 1, 0) + jnp.where(place > 0, 1, 0)
    pl.semaphore_wait(barrier, expected)

    @pl.when(place == last)
    def _():
        @pl.loop(0, micro)
        def _(m):
            pltpu.make_async_remote_copy(
                cot.at[m], g_in.at[m], c_send, g_recv.at[m], device_id=partner, device_id_type=MESH
            ).start()

    for copy in weights:
        copy.wait()

    def forward(m):
        pltpu.make_async_copy(x_in.at[m], x_in.at[m], x_recv.at[m]).wait()
        x = x_in[m]
        gate = jnp.dot(x, wg[...], preferred_element_type=F32)
        up = jnp.dot(x, wu[...], preferred_element_type=F32)
        xf = x.astype(F32)
        r = lax.rsqrt(jnp.mean(xf * xf, axis=-1, keepdims=True) + 1e-06)
        gate = gate * r
        up = up * r
        hidden = (gate * jax.nn.sigmoid(gate) * up).astype(BF16)
        gate_s[m] = gate
        up_s[m] = up
        hid_s[m] = hidden
        r_s[m] = jnp.broadcast_to(r, (r.shape[0], 128))

        @pl.when(place < last)
        def _():
            for k in range(CHUNKS):
                cols = slice(k * span, (k + 1) * span)
                branch = lax.dot_general(
                    hidden, wd[cols, :], LAST_LAST, preferred_element_type=F32
                )
                x_out[m, :, cols] = (x_in[m, :, cols].astype(F32) + branch).astype(BF16)
                pltpu.make_async_remote_copy(
                    x_out.at[m, :, cols],
                    x_in.at[m, :, cols],
                    x_send,
                    x_recv.at[m],
                    device_id=after,
                    device_id_type=MESH,
                ).start()

    def backward(m):
        pltpu.make_async_copy(g_in.at[m], g_in.at[m], g_recv.at[m]).wait()
        d_hidden = jnp.dot(g_in[m], wd[...], preferred_element_type=F32)
        gate = gate_s[m]
        up = up_s[m]
        r = r_s[m, :, 0:1]
        sig = jax.nn.sigmoid(gate)
        d_gate = d_hidden * up * sig * (1.0 + gate * (1.0 - sig))
        d_up = d_hidden * gate * sig
        dg = d_gate.astype(BF16)
        du = d_up.astype(BF16)
        inner = jnp.sum(
            dg.astype(F32) * gate + du.astype(F32) * up, axis=-1, keepdims=True
        ) * (1.0 / width)
        shrink = r * inner
        for k in range(CHUNKS):
            cols = slice(k * span, (k + 1) * span)
            normed_grad = lax.dot_general(dg, wg[cols, :], LAST_LAST, preferred_element_type=F32)
            normed_grad = normed_grad + lax.dot_general(
                du, wu[cols, :], LAST_LAST, preferred_element_type=F32
            )
            g_out[m, :, cols] = (
                g_in[m, :, cols].astype(F32)
                + r * (normed_grad - x_in[m, :, cols].astype(F32) * shrink)
            ).astype(BF16)

            @pl.when(place > 0)
            def _():
                pltpu.make_async_remote_copy(
                    g_out.at[m, :, cols],
                    g_in.at[m, :, cols],
                    g_send,
                    g_recv.at[m],
                    device_id=before,
                    device_id_type=MESH,
                ).start()

        @pl.when(upper)
        def _():
            pltpu.make_async_remote_copy(
                g_out.at[m],
                grad_in.at[m],
                o_send,
                o_recv,
                device_id=partner,
                device_id_type=MESH,
            ).start()

        @pl.when(jnp.logical_not(upper))
        def _():
            pltpu.make_async_copy(g_out.at[m], grad_in.at[m], o_recv).start()

        dg_s[m] = (d_gate * r).astype(BF16)
        du_s[m] = (d_up * r).astype(BF16)

    lead = jnp.minimum(1 + AHEAD * (last - place), micro)

    @pl.loop(0, micro + lead)
    def _(i):
        @pl.when(i >= lead)
        def _():
            backward(i - lead)

        @pl.when(i < micro)
        def _():
            forward(i)

    rows = micro * x_in.shape[1]
    tile = width // depth
    own = tile // 4
    dg_all = dg_s[...].reshape(rows, units)
    du_all = du_s[...].reshape(rows, units)
    hid_all = hid_s[...].reshape(rows, units)
    streams = ring_in.shape[0]
    stretch = 3 * units // streams

    def weight_terms(q):
        at = pl.multiple_of(q * tile, tile)
        xs = x_in[:, :, pl.ds(at, tile)].reshape(rows, tile)
        gs = g_in[:, :, pl.ds(at, tile)].reshape(rows, tile)
        for j, (left, right) in enumerate(((xs, dg_all), (xs, du_all), (gs, hid_all))):
            term = lax.dot_general(left, right, ROWS_ROWS, preferred_element_type=F32)
            part[q, :, :, :, j * units : (j + 1) * units] = term.astype(BF16).reshape(
                2, 2, own, units
            )
        for k in range(2):
            pltpu.make_async_remote_copy(
                part.at[q, k, 1 - core],
                from_core.at[q, k],
                core_send,
                core_recv.at[q],
                device_id=sibling,
                device_id_type=MESH,
            ).start()

    def chip_sum(q, cols):
        return part[q, :, core, :, cols].astype(F32) + from_core[q, :, :, cols].astype(F32)

    def both_ways(step):
        return (
            lax.rem(deep + 2 * depth - 1 - step, depth),
            lax.rem(deep + 1 + step, depth),
        )

    for q in both_ways(0):
        weight_terms(q)

    @pl.loop(0, depth - 1)
    def _(step):
        down, up = both_ways(step)

        @pl.when(step < depth // 2 - 1)
        def _():
            first, second = both_ways(step + 1)
            weight_terms(first)
            weight_terms(jnp.where(step == depth // 2 - 2, deep, second))

        @pl.when(step < depth // 2)
        def _():
            pltpu.make_async_copy(from_core.at[down], from_core.at[down], core_recv.at[down]).wait()

        @pl.when(step < depth // 2 - 1)
        def _():
            pltpu.make_async_copy(from_core.at[up], from_core.at[up], core_recv.at[up]).wait()

        for n in range(streams):
            q = (down, up)[n % 2]
            cols = slice(n * stretch, (n + 1) * stretch)
            total = chip_sum(q, cols)

            @pl.when(step == 0)
            def _():
                ring_out[n, step] = total.astype(BF16)

            @pl.when(step > 0)
            def _():
                pltpu.make_async_copy(
                    ring_in.at[n, step - 1], ring_in.at[n, step - 1], ring_recv.at[n, step - 1]
                ).wait()
                ring_out[n, step] = (total + ring_in[n, step - 1].astype(F32)).astype(BF16)

            pltpu.make_async_remote_copy(
                ring_out.at[n, step],
                ring_in.at[n, step],
                ring_send.at[n],
                ring_recv.at[n, step],
                device_id=ring_to[n % 2],
                device_id_type=MESH,
            ).start()

    pltpu.make_async_copy(from_core.at[deep], from_core.at[deep], core_recv.at[deep]).wait()
    end = depth - 2
    for n in range(streams):
        cols = slice(n * stretch, (n + 1) * stretch)
        pltpu.make_async_copy(ring_in.at[n, end], ring_in.at[n, end], ring_recv.at[n, end]).wait()
        side_out[n] = (
            part[deep, 1 - side, core, :, cols].astype(F32)
            + from_core[deep, 1 - side, :, cols].astype(F32)
            + ring_in[n, end, 1 - side].astype(F32)
        ).astype(BF16)
        pltpu.make_async_remote_copy(
            side_out.at[n],
            side_in.at[n],
            side_send,
            side_recv.at[n],
            device_id=partner,
            device_id_type=MESH,
        ).start()
    whole = []
    for n in range(streams):
        cols = slice(n * stretch, (n + 1) * stretch)
        pltpu.make_async_copy(side_in.at[n], side_in.at[n], side_recv.at[n]).wait()
        whole.append(
            part[deep, side, core, :, cols].astype(F32)
            + from_core[deep, side, :, cols].astype(F32)
            + ring_in[n, end, side].astype(F32)
            + side_in[n].astype(F32)
        )
    whole = jnp.concatenate(whole, axis=1)
    grad_g[...] = whole[:, :units]
    grad_u[...] = whole[:, units : 2 * units]
    grad_d[...] = whole[:, 2 * units :]

    pltpu.make_async_copy(side_out, side_out, side_send).wait()
    pltpu.make_async_copy(from_core, from_core, core_send).wait()
    for n in range(streams):
        pltpu.make_async_copy(ring_out.at[n], ring_out.at[n], ring_send.at[n]).wait()

    @pl.when(place < last)
    def _():
        pltpu.make_async_copy(x_out, x_out, x_send).wait()

    @pl.when(place > 0)
    def _():
        pltpu.make_async_copy(g_out, g_out, g_send).wait()

    @pl.when(place == last)
    def _():
        pltpu.make_async_copy(g_in, g_in, c_send).wait()

    @pl.when(upper)
    def _():
        pltpu.make_async_copy(g_out, g_out, o_send).wait()

    pltpu.make_async_copy(g_out, grad_in, o_recv).wait()


def run_pipeline(tokens, cotangent, w_gate, w_up, w_down):
    sections = lax.axis_size("section")
    tok_rows, width = tokens.shape
    units = w_gate.shape[1]
    micro = MICRO
    rows = tok_rows // micro
    anywhere = pl.BlockSpec(memory_space=pl.ANY)
    wide = pltpu.VMEM((micro, rows, width), BF16)
    slim = pltpu.VMEM((micro, rows, units), BF16)
    slim_f = pltpu.VMEM((micro, rows, units), F32)
    weight = pltpu.VMEM((width, units), BF16)
    dma = pltpu.SemaphoreType.DMA
    grad = jax.ShapeDtypeStruct((width // lax.axis_size(DP), units), F32)
    streams, depth = STREAMS, lax.axis_size("dp_0")
    own, stretch = width // (4 * depth), 3 * units // streams
    vmem = pl.BlockSpec(memory_space=pltpu.VMEM)
    grad_in, *grads = pl.pallas_call(
        functools.partial(pipeline_kernel, sections, micro),
        out_shape=(
            jax.ShapeDtypeStruct((micro, rows, width), BF16),
            grad,
            grad,
            grad,
        ),
        in_specs=[anywhere] * 5,
        out_specs=(anywhere, vmem, vmem, vmem),
        scratch_shapes=[
            weight,
            weight,
            weight,
            wide,
            wide,
            wide,
            wide,
            slim_f,
            slim_f,
            slim,
            slim,
            slim,
            pltpu.VMEM((micro, rows, 128), F32),
            pltpu.VMEM((depth, 2, 2, own, 3 * units), BF16),
            pltpu.VMEM((depth, 2, own, 3 * units), BF16),
            pltpu.VMEM((streams, depth - 1, 2, own, stretch), BF16),
            pltpu.VMEM((streams, depth - 1, 2, own, stretch), BF16),
            pltpu.VMEM((streams, own, stretch), BF16),
            pltpu.VMEM((streams, own, stretch), BF16),
            dma((3,)),
            dma((micro,)),
            dma((micro,)),
            dma,
            dma,
            dma,
            dma,
            dma,
            dma,
            dma((depth,)),
            dma((streams,)),
            dma((streams, depth - 1)),
            dma,
            dma((streams,)),
        ],
        compiler_params=pltpu.CompilerParams(
            collective_id=0, has_side_effects=True, vmem_limit_bytes=56 * 1024 * 1024
        ),
        name="pipeline",
    )(
        tokens.reshape(micro, rows, width),
        cotangent.reshape(micro, rows, width),
        w_gate,
        w_up,
        w_down,
    )
    return grad_in.reshape(tok_rows, width), *grads


def body(tokens, cotangent, w_gate, w_up, w_down):
    outs = run_pipeline(tokens, cotangent, w_gate[0], w_up[0], w_down[0])
    return tuple(out[None] for out in outs)


def solution(mesh):
    torus = Mesh(
        mesh.devices.reshape(mesh.shape["section"], 8, 2, 2), ("section", "dp_0", "dp_1", "dp_2")
    )
    placed = (
        P(DP, None),
        P(DP, None),
        P("section", None, None),
        P("section", None, None),
        P("section", None, None),
    )
    return jax.shard_map(
        body,
        mesh=torus,
        in_specs=placed,
        out_specs=(
            P("section", DP, None),
            P("section", DP, None),
            P("section", DP, None),
            P("section", DP, None),
        ),
        check_vma=False,
    )
```

```python
import functools

import jax
import jax.numpy as jnp
from jax import lax
from jax.experimental import pallas as pl
from jax.experimental.pallas import tpu as pltpu
from jax.sharding import Mesh
from jax.sharding import PartitionSpec as P

MICRO = 15
AHEAD = 4
CHUNKS = 2
STREAMS = 4
DP = ("dp_0", "dp_1", "dp_2")
MESH = pl.DeviceIdType.MESH
F32 = jnp.float32
BF16 = jnp.bfloat16
ROWS_ROWS = (((0,), (0,)), ((), ()))


def pipeline_kernel(
    sections,
    micro,
    tok,
    cot,
    wg_h,
    wu_h,
    wd_h,
    grad_in,
    grad_g,
    grad_u,
    grad_d,
    wg,
    wu,
    wd,
    wd_t,
    wgu_t,
    x_in,
    g_in,
    x_out,
    g_out,
    gate_s,
    up_s,
    hid_s,
    dgu_s,
    r_s,
    part,
    from_core,
    ring_in,
    ring_out,
    side_out,
    side_in,
    w_sem,
    turn,
    x_recv,
    g_recv,
    x_send,
    g_send,
    c_send,
    o_send,
    o_recv,
    core_send,
    core_recv,
    ring_send,
    ring_recv,
    side_send,
    side_recv,
):
    place = lax.axis_index("section")
    deep = lax.axis_index("dp_0")
    side = lax.axis_index("dp_1")
    core = lax.axis_index("dp_2")
    depth = part.shape[0]
    half = sections // 2
    last = sections - 1
    upper = place >= half
    width = x_in.shape[2]
    units = wg.shape[1]
    span = width // CHUNKS

    weights = [
        pltpu.make_async_copy(src, dst, w_sem.at[k])
        for k, (src, dst) in enumerate(((wd_h, wd), (wg_h, wg), (wu_h, wu)))
    ]
    for copy in weights:
        copy.start()

    @pl.when(place == 0)
    def _():
        @pl.loop(0, micro)
        def _(m):
            pltpu.make_async_copy(tok.at[m], x_in.at[m], x_recv.at[m]).start()

    next_side = jnp.where(place == half - 1, 1 - side, side)
    prev_side = jnp.where(place == half, 1 - side, side)
    after = {"section": lax.rem(place + 1, sections), "dp_1": next_side}
    before = {"section": lax.rem(place + sections - 1, sections), "dp_1": prev_side}
    partner = {"dp_1": 1 - side}
    sibling = {"dp_2": 1 - core}
    ring_to = ({"dp_0": lax.rem(deep + 1, depth)}, {"dp_0": lax.rem(deep + depth - 1, depth)})

    barrier = pltpu.get_barrier_semaphore()

    @pl.when(place < last)
    def _():
        pl.semaphore_signal(barrier, inc=1, device_id=after, device_id_type=MESH)

    @pl.when(place > 0)
    def _():
        pl.semaphore_signal(barrier, inc=1, device_id=before, device_id_type=MESH)

    for friend in (partner, sibling, *ring_to):
        pl.semaphore_signal(barrier, inc=1, device_id=friend, device_id_type=MESH)
    expected = 4 + jnp.where(place < last, 1, 0) + jnp.where(place > 0, 1, 0)
    pl.semaphore_wait(barrier, expected)

    @pl.when(place == last)
    def _():
        @pl.loop(0, micro)
        def _(m):
            pltpu.make_async_remote_copy(
                cot.at[m], g_in.at[m], c_send, g_recv.at[m], device_id=partner, device_id_type=MESH
            ).start()

    block = width // depth

    def turned(src, dst, base):
        @pl.loop(0, depth)
        def _(k):
            at = pl.multiple_of(k * block, block)
            dst[base : base + units, pl.ds(at, block)] = src[pl.ds(at, block), :].T

    def turn_gate_up():
        turned(wg, wgu_t, 0)
        turned(wu, wgu_t, units)

    weights[0].wait()
    turned(wd, wd_t, 0)
    weights[1].wait()
    weights[2].wait()

    @pl.when(place > 0)
    def _():
        turn_gate_up()

    def forward(m):
        pltpu.make_async_copy(x_in.at[m], x_in.at[m], x_recv.at[m]).wait()
        x = x_in[m]
        gate = jnp.dot(x, wg[...], preferred_element_type=F32)
        up = jnp.dot(x, wu[...], preferred_element_type=F32)
        xf = x.astype(F32)
        r = lax.rsqrt(jnp.mean(xf * xf, axis=-1, keepdims=True) + 1e-06)
        gate = gate * r
        up = up * r
        hidden = (gate * jax.nn.sigmoid(gate) * up).astype(BF16)
        gate_s[m] = gate
        up_s[m] = up
        hid_s[m] = hidden
        r_s[m] = jnp.broadcast_to(r, (r.shape[0], 128))

        @pl.when(place < last)
        def _():
            for k in range(CHUNKS):
                cols = slice(k * span, (k + 1) * span)
                branch = jnp.dot(hidden, wd_t[:, cols], preferred_element_type=F32)
                x_out[m, :, cols] = (x_in[m, :, cols].astype(F32) + branch).astype(BF16)
                pltpu.make_async_remote_copy(
                    x_out.at[m, :, cols],
                    x_in.at[m, :, cols],
                    x_send,
                    x_recv.at[m],
                    device_id=after,
                    device_id_type=MESH,
                ).start()

    def backward(m):
        pltpu.make_async_copy(g_in.at[m], g_in.at[m], g_recv.at[m]).wait()
        d_hidden = jnp.dot(g_in[m], wd[...], preferred_element_type=F32)
        gate = gate_s[m]
        up = up_s[m]
        r = r_s[m, :, 0:1]
        sig = jax.nn.sigmoid(gate)
        d_gate = d_hidden * up * sig * (1.0 + gate * (1.0 - sig))
        d_up = d_hidden * gate * sig
        dg = d_gate.astype(BF16)
        du = d_up.astype(BF16)
        inner = jnp.sum(
            dg.astype(F32) * gate + du.astype(F32) * up, axis=-1, keepdims=True
        ) * (1.0 / width)
        shrink = r * inner
        dgu = jnp.concatenate([dg, du], axis=1)
        for k in range(CHUNKS):
            cols = slice(k * span, (k + 1) * span)
            normed_grad = jnp.dot(dgu, wgu_t[:, cols], preferred_element_type=F32)
            g_out[m, :, cols] = (
                g_in[m, :, cols].astype(F32)
                + r * (normed_grad - x_in[m, :, cols].astype(F32) * shrink)
            ).astype(BF16)

            @pl.when(place > 0)
            def _():
                pltpu.make_async_remote_copy(
                    g_out.at[m, :, cols],
                    g_in.at[m, :, cols],
                    g_send,
                    g_recv.at[m],
                    device_id=before,
                    device_id_type=MESH,
                ).start()

        @pl.when(upper)
        def _():
            pltpu.make_async_remote_copy(
                g_out.at[m],
                grad_in.at[m],
                o_send,
                o_recv,
                device_id=partner,
                device_id_type=MESH,
            ).start()

        @pl.when(jnp.logical_not(upper))
        def _():
            pltpu.make_async_copy(g_out.at[m], grad_in.at[m], o_recv).start()

        dgu_s[m, :, :units] = (d_gate * r).astype(BF16)
        dgu_s[m, :, units:] = (d_up * r).astype(BF16)

    lead = jnp.minimum(1 + AHEAD * (last - place), micro)

    @pl.loop(0, micro + lead)
    def _(i):
        @pl.when((i == lead) & (place == 0))
        def _():
            turn_gate_up()

        @pl.when(i >= lead)
        def _():
            backward(i - lead)

        @pl.when((i == 0) & (place == 0) & (core == 1))
        def _():
            pl.semaphore_wait(turn, 1)

        @pl.when(i < micro)
        def _():
            forward(i)

        @pl.when((i == 0) & (place == 0) & (core == 0))
        def _():
            pl.semaphore_signal(turn, inc=1, device_id=sibling, device_id_type=MESH)

    rows = micro * x_in.shape[1]
    tile = width // depth
    own = tile // 4
    dgu_all = dgu_s[...].reshape(rows, 2 * units)
    hid_all = hid_s[...].reshape(rows, units)
    streams = ring_in.shape[0]
    stretch = 3 * units // streams

    def weight_terms(q):
        at = pl.multiple_of(q * tile, tile)
        xs = x_in[:, :, pl.ds(at, tile)].reshape(rows, tile)
        gs = g_in[:, :, pl.ds(at, tile)].reshape(rows, tile)
        for left, right, low in ((xs, dgu_all, 0), (gs, hid_all, 2 * units)):
            term = lax.dot_general(left, right, ROWS_ROWS, preferred_element_type=F32)
            high = low + right.shape[1]
            part[q, :, :, :, low:high] = term.astype(BF16).reshape(2, 2, own, high - low)
        for k in range(2):
            pltpu.make_async_remote_copy(
                part.at[q, k, 1 - core],
                from_core.at[q, k],
                core_send,
                core_recv.at[q],
                device_id=sibling,
                device_id_type=MESH,
            ).start()

    def chip_sum(q, cols):
        return part[q, :, core, :, cols].astype(F32) + from_core[q, :, :, cols].astype(F32)

    def both_ways(step):
        return (
            lax.rem(deep + 2 * depth - 1 - step, depth),
            lax.rem(deep + 1 + step, depth),
        )

    for q in both_ways(0):
        weight_terms(q)

    @pl.loop(0, depth - 1)
    def _(step):
        down, up = both_ways(step)

        @pl.when(step < depth // 2 - 1)
        def _():
            first, second = both_ways(step + 1)
            weight_terms(first)
            weight_terms(jnp.where(step == depth // 2 - 2, deep, second))

        @pl.when(step < depth // 2)
        def _():
            pltpu.make_async_copy(from_core.at[down], from_core.at[down], core_recv.at[down]).wait()

        @pl.when(step < depth // 2 - 1)
        def _():
            pltpu.make_async_copy(from_core.at[up], from_core.at[up], core_recv.at[up]).wait()

        for n in range(streams):
            q = (down, up)[n % 2]
            cols = slice(n * stretch, (n + 1) * stretch)
            total = chip_sum(q, cols)

            @pl.when(step == 0)
            def _():
                ring_out[n, step] = total.astype(BF16)

            @pl.when(step > 0)
            def _():
                pltpu.make_async_copy(
                    ring_in.at[n, step - 1], ring_in.at[n, step - 1], ring_recv.at[n, step - 1]
                ).wait()
                ring_out[n, step] = (total + ring_in[n, step - 1].astype(F32)).astype(BF16)

            pltpu.make_async_remote_copy(
                ring_out.at[n, step],
                ring_in.at[n, step],
                ring_send.at[n],
                ring_recv.at[n, step],
                device_id=ring_to[n % 2],
                device_id_type=MESH,
            ).start()

    pltpu.make_async_copy(from_core.at[deep], from_core.at[deep], core_recv.at[deep]).wait()
    end = depth - 2
    for n in range(streams):
        cols = slice(n * stretch, (n + 1) * stretch)
        pltpu.make_async_copy(ring_in.at[n, end], ring_in.at[n, end], ring_recv.at[n, end]).wait()
        side_out[n] = (
            part[deep, 1 - side, core, :, cols].astype(F32)
            + from_core[deep, 1 - side, :, cols].astype(F32)
            + ring_in[n, end, 1 - side].astype(F32)
        ).astype(BF16)
        pltpu.make_async_remote_copy(
            side_out.at[n],
            side_in.at[n],
            side_send,
            side_recv.at[n],
            device_id=partner,
            device_id_type=MESH,
        ).start()
    whole = []
    for n in range(streams):
        cols = slice(n * stretch, (n + 1) * stretch)
        pltpu.make_async_copy(side_in.at[n], side_in.at[n], side_recv.at[n]).wait()
        whole.append(
            part[deep, side, core, :, cols].astype(F32)
            + from_core[deep, side, :, cols].astype(F32)
            + ring_in[n, end, side].astype(F32)
            + side_in[n].astype(F32)
        )
    whole = jnp.concatenate(whole, axis=1)
    grad_g[...] = whole[:, :units]
    grad_u[...] = whole[:, units : 2 * units]
    grad_d[...] = whole[:, 2 * units :]

    pltpu.make_async_copy(side_out, side_out, side_send).wait()
    pltpu.make_async_copy(from_core, from_core, core_send).wait()
    for n in range(streams):
        pltpu.make_async_copy(ring_out.at[n], ring_out.at[n], ring_send.at[n]).wait()

    @pl.when(place < last)
    def _():
        pltpu.make_async_copy(x_out, x_out, x_send).wait()

    @pl.when(place > 0)
    def _():
        pltpu.make_async_copy(g_out, g_out, g_send).wait()

    @pl.when(place == last)
    def _():
        pltpu.make_async_copy(g_in, g_in, c_send).wait()

    @pl.when(upper)
    def _():
        pltpu.make_async_copy(g_out, g_out, o_send).wait()

    pltpu.make_async_copy(g_out, grad_in, o_recv).wait()


def run_pipeline(tokens, cotangent, w_gate, w_up, w_down):
    sections = lax.axis_size("section")
    tok_rows, width = tokens.shape
    units = w_gate.shape[1]
    micro = MICRO
    rows = tok_rows // micro
    anywhere = pl.BlockSpec(memory_space=pl.ANY)
    wide = pltpu.VMEM((micro, rows, width), BF16)
    slim = pltpu.VMEM((micro, rows, units), BF16)
    slim_f = pltpu.VMEM((micro, rows, units), F32)
    weight = pltpu.VMEM((width, units), BF16)
    dma = pltpu.SemaphoreType.DMA
    grad = jax.ShapeDtypeStruct((width // lax.axis_size(DP), units), F32)
    streams, depth = STREAMS, lax.axis_size("dp_0")
    own, stretch = width // (4 * depth), 3 * units // streams
    vmem = pl.BlockSpec(memory_space=pltpu.VMEM)
    grad_in, *grads = pl.pallas_call(
        functools.partial(pipeline_kernel, sections, micro),
        out_shape=(
            jax.ShapeDtypeStruct((micro, rows, width), BF16),
            grad,
            grad,
            grad,
        ),
        in_specs=[anywhere] * 5,
        out_specs=(anywhere, vmem, vmem, vmem),
        scratch_shapes=[
            weight,
            weight,
            weight,
            pltpu.VMEM((units, width), BF16),
            pltpu.VMEM((2 * units, width), BF16),
            wide,
            wide,
            wide,
            wide,
            slim_f,
            slim_f,
            slim,
            pltpu.VMEM((micro, rows, 2 * units), BF16),
            pltpu.VMEM((micro, rows, 128), F32),
            pltpu.VMEM((depth, 2, 2, own, 3 * units), BF16),
            pltpu.VMEM((depth, 2, own, 3 * units), BF16),
            pltpu.VMEM((streams, depth - 1, 2, own, stretch), BF16),
            pltpu.VMEM((streams, depth - 1, 2, own, stretch), BF16),
            pltpu.VMEM((streams, own, stretch), BF16),
            pltpu.VMEM((streams, own, stretch), BF16),
            dma((3,)),
            pltpu.SemaphoreType.REGULAR,
            dma((micro,)),
            dma((micro,)),
            dma,
            dma,
            dma,
            dma,
            dma,
            dma,
            dma((depth,)),
            dma((streams,)),
            dma((streams, depth - 1)),
            dma,
            dma((streams,)),
        ],
        compiler_params=pltpu.CompilerParams(
            collective_id=0, has_side_effects=True, vmem_limit_bytes=56 * 1024 * 1024
        ),
        name="pipeline",
    )(
        tokens.reshape(micro, rows, width),
        cotangent.reshape(micro, rows, width),
        w_gate,
        w_up,
        w_down,
    )
    return grad_in.reshape(tok_rows, width), *grads


def body(tokens, cotangent, w_gate, w_up, w_down):
    outs = run_pipeline(tokens, cotangent, w_gate[0], w_up[0], w_down[0])
    return tuple(out[None] for out in outs)


def solution(mesh):
    torus = Mesh(
        mesh.devices.reshape(mesh.shape["section"], 8, 2, 2), ("section", "dp_0", "dp_1", "dp_2")
    )
    placed = (
        P(DP, None),
        P(DP, None),
        P("section", None, None),
        P("section", None, None),
        P("section", None, None),
    )
    return jax.shard_map(
        body,
        mesh=torus,
        in_specs=placed,
        out_specs=(
            P("section", DP, None),
            P("section", DP, None),
            P("section", DP, None),
            P("section", DP, None),
        ),
        check_vma=False,
    )
```

```python
import functools

import jax
import jax.numpy as jnp
from jax import lax
from jax.experimental import pallas as pl
from jax.experimental.pallas import tpu as pltpu
from jax.sharding import Mesh
from jax.sharding import PartitionSpec as P

MICRO = 15
AHEAD = 4
CHUNKS = 2
STREAMS = 4
SIDE_FIRST = 2
PIECES = 5
DP = ("dp_0", "dp_1", "dp_2")
MESH = pl.DeviceIdType.MESH
F32 = jnp.float32
BF16 = jnp.bfloat16
ROWS_ROWS = (((0,), (0,)), ((), ()))


def pipeline_kernel(
    sections,
    micro,
    tok,
    cot,
    wg_h,
    wu_h,
    wd_h,
    grad_in,
    grad_g,
    grad_u,
    grad_d,
    wg,
    wu,
    wd,
    wd_t,
    wgu_t,
    x_in,
    g_in,
    x_out,
    g_out,
    gate_s,
    up_s,
    hid_s,
    dgu_s,
    r_s,
    part,
    from_core,
    ring_in,
    ring_out,
    side_out,
    side_in,
    end_out,
    end_in,
    w_sem,
    turn,
    x_recv,
    g_recv,
    x_send,
    g_send,
    c_send,
    o_send,
    o_recv,
    core_send,
    core_recv,
    ring_send,
    ring_recv,
    side_send,
    side_recv,
    end_send,
    end_recv,
):
    place = lax.axis_index("section")
    deep = lax.axis_index("dp_0")
    side = lax.axis_index("dp_1")
    core = lax.axis_index("dp_2")
    depth = part.shape[0]
    half = sections // 2
    last = sections - 1
    upper = place >= half
    width = x_in.shape[2]
    units = wg.shape[1]
    span = width // CHUNKS
    chunks = [slice(k * span, (k + 1) * span) for k in range(CHUNKS)]

    weights = [
        pltpu.make_async_copy(src, dst, w_sem.at[k])
        for k, (src, dst) in enumerate(((wd_h, wd), (wg_h, wg), (wu_h, wu)))
    ]
    for copy in weights:
        copy.start()

    @pl.when(place == 0)
    def _():
        @pl.loop(0, micro)
        def _(m):
            pltpu.make_async_copy(tok.at[m], x_in.at[m], x_recv.at[m]).start()

    next_side = jnp.where(place == half - 1, 1 - side, side)
    prev_side = jnp.where(place == half, 1 - side, side)
    after = {"section": lax.rem(place + 1, sections), "dp_1": next_side}
    before = {"section": lax.rem(place + sections - 1, sections), "dp_1": prev_side}
    partner = {"dp_1": 1 - side}
    sibling = {"dp_2": 1 - core}
    ring_to = ({"dp_0": lax.rem(deep + 1, depth)}, {"dp_0": lax.rem(deep + depth - 1, depth)})

    barrier = pltpu.get_barrier_semaphore()

    @pl.when(place < last)
    def _():
        pl.semaphore_signal(barrier, inc=1, device_id=after, device_id_type=MESH)

    @pl.when(place > 0)
    def _():
        pl.semaphore_signal(barrier, inc=1, device_id=before, device_id_type=MESH)

    for friend in (partner, sibling, *ring_to):
        pl.semaphore_signal(barrier, inc=1, device_id=friend, device_id_type=MESH)
    expected = 4 + jnp.where(place < last, 1, 0) + jnp.where(place > 0, 1, 0)
    pl.semaphore_wait(barrier, expected)

    @pl.when(place == last)
    def _():
        @pl.loop(0, micro)
        def _(m):
            pltpu.make_async_remote_copy(
                cot.at[m], g_in.at[m], c_send, g_recv.at[m], device_id=partner, device_id_type=MESH
            ).start()

    block = width // depth

    def turned(src, dst, base):
        @pl.loop(0, depth)
        def _(k):
            at = pl.multiple_of(k * block, block)
            dst[base : base + units, pl.ds(at, block)] = src[pl.ds(at, block), :].T

    def turn_gate_up():
        turned(wg, wgu_t, 0)
        turned(wu, wgu_t, units)

    weights[0].wait()
    turned(wd, wd_t, 0)
    weights[1].wait()
    weights[2].wait()

    @pl.when(place > 0)
    def _():
        turn_gate_up()

    def forward(m):
        pltpu.make_async_copy(x_in.at[m], x_in.at[m], x_recv.at[m]).wait()
        x = x_in[m]
        gate = jnp.dot(x, wg[...], preferred_element_type=F32)
        up = jnp.dot(x, wu[...], preferred_element_type=F32)
        xf = x.astype(F32)
        r = lax.rsqrt(jnp.mean(xf * xf, axis=-1, keepdims=True) + 1e-06)
        gate = gate * r
        up = up * r
        hidden = (gate * jax.nn.sigmoid(gate) * up).astype(BF16)
        gate_s[m] = gate
        up_s[m] = up
        hid_s[m] = hidden
        r_s[m] = jnp.broadcast_to(r, (r.shape[0], 128))

        @pl.when(place < last)
        def _():
            for k, cols in enumerate(chunks):
                branch = jnp.dot(hidden, wd_t[:, cols], preferred_element_type=F32)
                x_out[m, :, cols] = (x_in[m, :, cols].astype(F32) + branch).astype(BF16)
                pltpu.make_async_remote_copy(
                    x_out.at[m, :, cols],
                    x_in.at[m, :, cols],
                    x_send,
                    x_recv.at[m],
                    device_id=after,
                    device_id_type=MESH,
                ).start()

    def backward(m):
        pltpu.make_async_copy(g_in.at[m], g_in.at[m], g_recv.at[m]).wait()
        d_hidden = jnp.dot(g_in[m], wd[...], preferred_element_type=F32)
        gate = gate_s[m]
        up = up_s[m]
        r = r_s[m, :, 0:1]
        sig = jax.nn.sigmoid(gate)
        d_gate = d_hidden * up * sig * (1.0 + gate * (1.0 - sig))
        d_up = d_hidden * gate * sig
        dg = d_gate.astype(BF16)
        du = d_up.astype(BF16)
        inner = jnp.sum(
            dg.astype(F32) * gate + du.astype(F32) * up, axis=-1, keepdims=True
        ) * (1.0 / width)
        shrink = r * inner
        dgu = jnp.concatenate([dg, du], axis=1)
        for k, cols in enumerate(chunks):
            normed_grad = jnp.dot(dgu, wgu_t[:, cols], preferred_element_type=F32)
            g_out[m, :, cols] = (
                g_in[m, :, cols].astype(F32)
                + r * (normed_grad - x_in[m, :, cols].astype(F32) * shrink)
            ).astype(BF16)

            @pl.when(place > 0)
            def _():
                pltpu.make_async_remote_copy(
                    g_out.at[m, :, cols],
                    g_in.at[m, :, cols],
                    g_send,
                    g_recv.at[m],
                    device_id=before,
                    device_id_type=MESH,
                ).start()

        @pl.when(upper)
        def _():
            pltpu.make_async_remote_copy(
                g_out.at[m],
                grad_in.at[m],
                o_send,
                o_recv,
                device_id=partner,
                device_id_type=MESH,
            ).start()

        @pl.when(jnp.logical_not(upper))
        def _():
            pltpu.make_async_copy(g_out.at[m], grad_in.at[m], o_recv).start()

        dgu_s[m, :, :units] = (d_gate * r).astype(BF16)
        dgu_s[m, :, units:] = (d_up * r).astype(BF16)

    lead = jnp.minimum(1 + AHEAD * (last - place), micro)

    @pl.loop(0, micro + lead)
    def _(i):
        @pl.when((i == lead) & (place == 0))
        def _():
            turn_gate_up()

        @pl.when(i >= lead)
        def _():
            backward(i - lead)

        @pl.when((i == 0) & (place == 0) & (core == 1))
        def _():
            pl.semaphore_wait(turn, 1)

        @pl.when(i < micro)
        def _():
            forward(i)

        @pl.when((i == 0) & (place == 0) & (core == 0))
        def _():
            pl.semaphore_signal(turn, inc=1, device_id=sibling, device_id_type=MESH)

    rows = micro * x_in.shape[1]
    tile = width // depth
    own = tile // 4
    dgu_all = dgu_s[...].reshape(rows, 2 * units)
    hid_all = hid_s[...].reshape(rows, units)
    streams, stretch = ring_in.shape[0], ring_in.shape[-1]
    first_b = SIDE_FIRST
    middle = depth // 2

    def tile_at(j):
        turn_off = jnp.where(lax.rem(j, 2) == 1, middle - (j + 1) // 2, j // 2 + middle)
        return lax.rem(deep + jnp.where(j == depth - 1, 0, turn_off), depth)

    def weight_terms(j):
        q = tile_at(j)
        at = pl.multiple_of(q * tile, tile)
        xs = x_in[:, :, pl.ds(at, tile)].reshape(rows, tile)
        gs = g_in[:, :, pl.ds(at, tile)].reshape(rows, tile)
        for left, right, low in ((xs, dgu_all, 0), (gs, hid_all, 2 * units)):
            term = lax.dot_general(left, right, ROWS_ROWS, preferred_element_type=F32)
            high = low + right.shape[1]
            part[q, :, :, :, low:high] = term.astype(BF16).reshape(2, 2, own, high - low)
        for k in range(2):
            pltpu.make_async_remote_copy(
                part.at[q, k, 1 - core],
                from_core.at[q, k],
                core_send,
                core_recv.at[q],
                device_id=sibling,
                device_id_type=MESH,
            ).start()

    def terms(low, high):
        @pl.loop(low, high)
        def _(j):
            weight_terms(j)

    def columns(n):
        return slice(n * stretch, (n + 1) * stretch)

    def chip_sum(q, k, cols):
        return part[q, k, core, :, cols].astype(F32) + from_core[q, k, :, cols].astype(F32)

    side_cols = slice(0, first_b * stretch)

    def chip_ready(j):
        q = tile_at(j)
        pltpu.make_async_copy(from_core.at[q], from_core.at[q], core_recv.at[q]).wait()
        side_out[q] = chip_sum(q, 1 - side, side_cols).astype(BF16)
        pltpu.make_async_remote_copy(
            side_out.at[q],
            side_in.at[q],
            side_send,
            side_recv.at[q],
            device_id=partner,
            device_id_type=MESH,
        ).start()

    def side_ready(j):
        q = tile_at(j)
        pltpu.make_async_copy(side_in.at[q], side_in.at[q], side_recv.at[q]).wait()

    def own_sums(n, q):
        if n < first_b:
            return [(0, chip_sum(q, side, columns(n)) + side_in[q, :, columns(n)].astype(F32))]
        return [(k, chip_sum(q, k, columns(n))) for k in range(2)]

    def slot(ref, n, way, step):
        return ref.at[n, way, step, 0] if n < first_b else ref.at[n, way, step]

    def ring_wait(n, way, step):
        ref = slot(ring_in, n, way, step)
        pltpu.make_async_copy(ref, ref, ring_recv.at[n, way, step]).wait()

    def ring_step(step, group):
        for long in (True, False):
            for n in group:
                for way in range(2):
                    if (n % 2 == way) != long or (step == 0 and not long):
                        continue
                    q = lax.rem(deep + (middle - step if way == 0 else middle + step), depth)
                    held = step > (0 if long else 1)
                    if held:
                        ring_wait(n, way, step - 1)
                    for k, total in own_sums(n, q):
                        if held:
                            total = total + ring_in[n, way, step - 1, k].astype(F32)
                        ring_out[n, way, step, k] = total.astype(BF16)
                    pltpu.make_async_remote_copy(
                        slot(ring_out, n, way, step),
                        slot(ring_in, n, way, step),
                        ring_send.at[n, way],
                        ring_recv.at[n, way, step],
                        device_id=ring_to[way],
                        device_id_type=MESH,
                    ).start()

    def arrived(n, k):
        return ring_in[n, 0, middle - 1, k].astype(F32) + ring_in[n, 1, middle - 1, k].astype(F32)

    group_a, group_b = range(first_b), range(first_b, streams)
    terms(0, 2)
    chip_ready(0)
    ring_step(0, group_b)
    terms(2, 4)
    chip_ready(1)
    chip_ready(2)
    ring_step(1, group_b)
    terms(4, 6)
    chip_ready(3)
    chip_ready(4)
    side_ready(0)
    ring_step(0, group_a)
    ring_step(2, group_b)
    terms(6, 8)
    chip_ready(5)
    chip_ready(6)
    side_ready(1)
    side_ready(2)
    ring_step(1, group_a)
    ring_step(3, group_b)
    chip_ready(7)
    side_ready(3)
    side_ready(4)
    ring_step(2, group_a)
    for n in group_b:
        for way in range(2):
            ring_wait(n, way, middle - 1)
        end_out[n - first_b] = (
            chip_sum(deep, 1 - side, columns(n)) + arrived(n, 1 - side)
        ).astype(BF16)
        pltpu.make_async_remote_copy(
            end_out.at[n - first_b],
            end_in.at[n - first_b],
            end_send,
            end_recv.at[n - first_b],
            device_id=partner,
            device_id_type=MESH,
        ).start()
    side_ready(5)
    side_ready(6)
    ring_step(3, group_a)
    side_ready(7)
    whole = {}
    for n in group_b:
        ref = end_in.at[n - first_b]
        pltpu.make_async_copy(ref, ref, end_recv.at[n - first_b]).wait()
        whole[n] = (
            chip_sum(deep, side, columns(n))
            + arrived(n, side)
            + end_in[n - first_b].astype(F32)
        )
    for n in group_a:
        for way in range(2):
            ring_wait(n, way, middle - 1)
        whole[n] = own_sums(n, deep)[0][1] + arrived(n, 0)
    whole = jnp.concatenate([whole[n] for n in range(streams)], axis=1)
    grad_g[...] = whole[:, :units]
    grad_u[...] = whole[:, units : 2 * units]
    grad_d[...] = whole[:, 2 * units :]

    pltpu.make_async_copy(side_out, side_out, side_send).wait()
    pltpu.make_async_copy(end_out, end_out, end_send).wait()
    pltpu.make_async_copy(from_core, from_core, core_send).wait()
    for n in range(streams):
        for way in range(2):
            lowest = 0 if n % 2 == way else 1
            sent = ring_out.at[n, way, lowest:middle]
            if n < first_b:
                sent = ring_out.at[n, way, lowest:middle, 0]
            pltpu.make_async_copy(sent, sent, ring_send.at[n, way]).wait()

    @pl.when(place < last)
    def _():
        pltpu.make_async_copy(x_out, x_out, x_send).wait()

    @pl.when(place > 0)
    def _():
        pltpu.make_async_copy(g_out, g_out, g_send).wait()

    @pl.when(place == last)
    def _():
        pltpu.make_async_copy(g_in, g_in, c_send).wait()

    @pl.when(upper)
    def _():
        pltpu.make_async_copy(g_out, g_out, o_send).wait()

    pltpu.make_async_copy(g_out, grad_in, o_recv).wait()


def finish_kernel(wide_in, g_in, u_in, d_in, wide_out, g_out, u_out, d_out, wide, slim, into, out):
    size = wide.shape[0] // PIECES
    routes = [
        (wide_in.at[pl.ds(k * size, size)], wide.at[pl.ds(k * size, size)],
         wide_out.at[pl.ds(k * size, size)])
        for k in range(PIECES)
    ]
    for k, (src, dst) in enumerate(((g_in, g_out), (u_in, u_out), (d_in, d_out))):
        routes.append((src, slim.at[k], dst))
    for k, (src, held, _) in enumerate(routes):
        pltpu.make_async_copy(src, held, into.at[k]).start()
    for k, (src, held, dst) in enumerate(routes):
        pltpu.make_async_copy(src, held, into.at[k]).wait()
        pltpu.make_async_copy(held, dst, out.at[k]).start()
    for k, (_, held, dst) in enumerate(routes):
        pltpu.make_async_copy(held, dst, out.at[k]).wait()


def finished(wide, *slim):
    anywhere = pl.BlockSpec(memory_space=pl.ANY)
    arrays = (wide, *slim)
    return pl.pallas_call(
        finish_kernel,
        out_shape=tuple(jax.ShapeDtypeStruct(a.shape, a.dtype) for a in arrays),
        in_specs=[anywhere] * 4,
        out_specs=(anywhere,) * 4,
        scratch_shapes=[
            pltpu.VMEM(wide.shape, wide.dtype),
            pltpu.VMEM((3, *slim[0].shape), F32),
            pltpu.SemaphoreType.DMA((PIECES + 3,)),
            pltpu.SemaphoreType.DMA((PIECES + 3,)),
        ],
        compiler_params=pltpu.CompilerParams(vmem_limit_bytes=60 * 1024 * 1024),
        name="finish",
    )(*arrays)


def run_pipeline(tokens, cotangent, w_gate, w_up, w_down):
    sections = lax.axis_size("section")
    tok_rows, width = tokens.shape
    units = w_gate.shape[1]
    micro = MICRO
    rows = tok_rows // micro
    anywhere = pl.BlockSpec(memory_space=pl.ANY)
    wide = pltpu.VMEM((micro, rows, width), BF16)
    slim = pltpu.VMEM((micro, rows, units), BF16)
    slim_f = pltpu.VMEM((micro, rows, units), F32)
    weight = pltpu.VMEM((width, units), BF16)
    dma = pltpu.SemaphoreType.DMA
    grad = jax.ShapeDtypeStruct((width // lax.axis_size(DP), units), F32)
    streams, depth = STREAMS, lax.axis_size("dp_0")
    own, stretch = width // (4 * depth), 3 * units // streams
    vmem = pl.BlockSpec(memory_space=pltpu.VMEM)
    grad_in, *grads = pl.pallas_call(
        functools.partial(pipeline_kernel, sections, micro),
        out_shape=(
            jax.ShapeDtypeStruct((micro, rows, width), BF16),
            grad,
            grad,
            grad,
        ),
        in_specs=[anywhere] * 5,
        out_specs=(anywhere, vmem, vmem, vmem),
        scratch_shapes=[
            weight,
            weight,
            weight,
            pltpu.VMEM((units, width), BF16),
            pltpu.VMEM((2 * units, width), BF16),
            wide,
            wide,
            wide,
            wide,
            slim_f,
            slim_f,
            slim,
            pltpu.VMEM((micro, rows, 2 * units), BF16),
            pltpu.VMEM((micro, rows, 128), F32),
            pltpu.VMEM((depth, 2, 2, own, 3 * units), BF16),
            pltpu.VMEM((depth, 2, own, 3 * units), BF16),
            pltpu.VMEM((streams, 2, depth // 2, 2, own, stretch), BF16),
            pltpu.VMEM((streams, 2, depth // 2, 2, own, stretch), BF16),
            pltpu.VMEM((depth, own, SIDE_FIRST * stretch), BF16),
            pltpu.VMEM((depth, own, SIDE_FIRST * stretch), BF16),
            pltpu.VMEM((streams - SIDE_FIRST, own, stretch), BF16),
            pltpu.VMEM((streams - SIDE_FIRST, own, stretch), BF16),
            dma((3,)),
            pltpu.SemaphoreType.REGULAR,
            dma((micro,)),
            dma((micro,)),
            dma,
            dma,
            dma,
            dma,
            dma,
            dma,
            dma((depth,)),
            dma((streams, 2)),
            dma((streams, 2, depth // 2)),
            dma,
            dma((depth,)),
            dma,
            dma((streams - SIDE_FIRST,)),
        ],
        compiler_params=pltpu.CompilerParams(
            collective_id=0, has_side_effects=True, vmem_limit_bytes=56 * 1024 * 1024
        ),
        name="pipeline",
    )(
        tokens.reshape(micro, rows, width),
        cotangent.reshape(micro, rows, width),
        w_gate,
        w_up,
        w_down,
    )
    return finished(grad_in.reshape(tok_rows, width), *grads)


def body(tokens, cotangent, w_gate, w_up, w_down):
    outs = run_pipeline(tokens, cotangent, w_gate[0], w_up[0], w_down[0])
    return tuple(out[None] for out in outs)


def solution(mesh):
    torus = Mesh(
        mesh.devices.reshape(mesh.shape["section"], 8, 2, 2), ("section", "dp_0", "dp_1", "dp_2")
    )
    placed = (
        P(DP, None),
        P(DP, None),
        P("section", None, None),
        P("section", None, None),
        P("section", None, None),
    )
    return jax.shard_map(
        body,
        mesh=torus,
        in_specs=placed,
        out_specs=(
            P("section", DP, None),
            P("section", DP, None),
            P("section", DP, None),
            P("section", DP, None),
        ),
        check_vma=False,
    )
```

```python
import functools

import jax
import jax.numpy as jnp
from jax import lax
from jax.experimental import pallas as pl
from jax.experimental.pallas import tpu as pltpu
from jax.sharding import Mesh
from jax.sharding import PartitionSpec as P

MICRO = 15
AHEAD = 4
CHUNKS = 2
STREAMS = 4
SIDE_FIRST = 2
PIECES = 5
DP = ("dp_0", "dp_1", "dp_2")
MESH = pl.DeviceIdType.MESH
F32 = jnp.float32
BF16 = jnp.bfloat16
ROWS_ROWS = (((0,), (0,)), ((), ()))


def pipeline_kernel(
    sections,
    micro,
    tok,
    cot,
    wg_h,
    wu_h,
    wd_h,
    grad_in,
    grad_g,
    grad_u,
    grad_d,
    wg,
    wu,
    wd,
    wd_t,
    wgu_t,
    x_in,
    g_in,
    x_out,
    g_out,
    gate_s,
    up_s,
    hid_s,
    dgu_s,
    r_s,
    part,
    from_core,
    ring_in,
    ring_out,
    side_out,
    side_in,
    end_out,
    end_in,
    w_sem,
    turn,
    x_recv,
    g_recv,
    x_send,
    g_send,
    c_send,
    o_send,
    o_recv,
    core_send,
    core_recv,
    ring_send,
    ring_recv,
    side_send,
    side_recv,
    end_send,
    end_recv,
):
    place = lax.axis_index("section")
    deep = lax.axis_index("dp_0")
    side = lax.axis_index("dp_1")
    core = lax.axis_index("dp_2")
    depth = part.shape[0]
    half = sections // 2
    last = sections - 1
    upper = place >= half
    width = x_in.shape[2]
    units = wg.shape[1]
    span = width // CHUNKS
    chunks = [slice(k * span, (k + 1) * span) for k in range(CHUNKS)]

    weights = [
        pltpu.make_async_copy(src, dst, w_sem.at[k])
        for k, (src, dst) in enumerate(((wd_h, wd), (wg_h, wg), (wu_h, wu)))
    ]
    for copy in weights:
        copy.start()

    @pl.when(place == 0)
    def _():
        @pl.loop(0, micro)
        def _(m):
            pltpu.make_async_copy(tok.at[m], x_in.at[m], x_recv.at[m]).start()

    next_side = jnp.where(place == half - 1, 1 - side, side)
    prev_side = jnp.where(place == half, 1 - side, side)
    after = {"section": lax.rem(place + 1, sections), "dp_1": next_side}
    before = {"section": lax.rem(place + sections - 1, sections), "dp_1": prev_side}
    partner = {"dp_1": 1 - side}
    sibling = {"dp_2": 1 - core}
    ring_to = ({"dp_0": lax.rem(deep + 1, depth)}, {"dp_0": lax.rem(deep + depth - 1, depth)})

    barrier = pltpu.get_barrier_semaphore()

    @pl.when(place < last)
    def _():
        pl.semaphore_signal(barrier, inc=1, device_id=after, device_id_type=MESH)

    @pl.when(place > 0)
    def _():
        pl.semaphore_signal(barrier, inc=1, device_id=before, device_id_type=MESH)

    for friend in (partner, sibling, *ring_to):
        pl.semaphore_signal(barrier, inc=1, device_id=friend, device_id_type=MESH)
    block = width // depth

    def turned(src, dst, base):
        @pl.loop(0, depth)
        def _(k):
            at = pl.multiple_of(k * block, block)
            dst[base : base + units, pl.ds(at, block)] = src[pl.ds(at, block), :].T

    def turn_gate_up():
        turned(wg, wgu_t, 0)
        turned(wu, wgu_t, units)

    weights[0].wait()
    turned(wd, wd_t, 0)
    expected = 4 + jnp.where(place < last, 1, 0) + jnp.where(place > 0, 1, 0)
    pl.semaphore_wait(barrier, expected)

    @pl.when(place == last)
    def _():
        @pl.loop(0, micro)
        def _(m):
            pltpu.make_async_remote_copy(
                cot.at[m], g_in.at[m], c_send, g_recv.at[m], device_id=partner, device_id_type=MESH
            ).start()

    weights[1].wait()
    weights[2].wait()

    @pl.when(place > 0)
    def _():
        turn_gate_up()

    def forward(m):
        pltpu.make_async_copy(x_in.at[m], x_in.at[m], x_recv.at[m]).wait()
        x = x_in[m]
        gate = jnp.dot(x, wg[...], preferred_element_type=F32)
        up = jnp.dot(x, wu[...], preferred_element_type=F32)
        xf = x.astype(F32)
        r = lax.rsqrt(jnp.mean(xf * xf, axis=-1, keepdims=True) + 1e-06)
        gate = gate * r
        up = up * r
        hidden = (gate * jax.nn.sigmoid(gate) * up).astype(BF16)
        gate_s[m] = gate
        up_s[m] = up
        hid_s[m] = hidden
        r_s[m] = jnp.broadcast_to(r, (r.shape[0], 128))

        @pl.when(place < last)
        def _():
            for k, cols in enumerate(chunks):
                branch = jnp.dot(hidden, wd_t[:, cols], preferred_element_type=F32)
                x_out[m, :, cols] = (x_in[m, :, cols].astype(F32) + branch).astype(BF16)
                pltpu.make_async_remote_copy(
                    x_out.at[m, :, cols],
                    x_in.at[m, :, cols],
                    x_send,
                    x_recv.at[m],
                    device_id=after,
                    device_id_type=MESH,
                ).start()

    def backward(m):
        pltpu.make_async_copy(g_in.at[m], g_in.at[m], g_recv.at[m]).wait()
        d_hidden = jnp.dot(g_in[m], wd[...], preferred_element_type=F32)
        gate = gate_s[m]
        up = up_s[m]
        r = r_s[m, :, 0:1]
        sig = jax.nn.sigmoid(gate)
        d_gate = d_hidden * up * sig * (1.0 + gate * (1.0 - sig))
        d_up = d_hidden * gate * sig
        dg = d_gate.astype(BF16)
        du = d_up.astype(BF16)
        inner = jnp.sum(
            dg.astype(F32) * gate + du.astype(F32) * up, axis=-1, keepdims=True
        ) * (1.0 / width)
        shrink = r * inner
        dgu = jnp.concatenate([dg, du], axis=1)
        for k, cols in enumerate(chunks):
            normed_grad = jnp.dot(dgu, wgu_t[:, cols], preferred_element_type=F32)
            g_out[m, :, cols] = (
                g_in[m, :, cols].astype(F32)
                + r * (normed_grad - x_in[m, :, cols].astype(F32) * shrink)
            ).astype(BF16)

            @pl.when(place > 0)
            def _():
                pltpu.make_async_remote_copy(
                    g_out.at[m, :, cols],
                    g_in.at[m, :, cols],
                    g_send,
                    g_recv.at[m],
                    device_id=before,
                    device_id_type=MESH,
                ).start()

        @pl.when(upper)
        def _():
            pltpu.make_async_remote_copy(
                g_out.at[m],
                grad_in.at[m],
                o_send,
                o_recv,
                device_id=partner,
                device_id_type=MESH,
            ).start()

        @pl.when(jnp.logical_not(upper))
        def _():
            pltpu.make_async_copy(g_out.at[m], grad_in.at[m], o_recv).start()

        dgu_s[m, :, :units] = (d_gate * r).astype(BF16)
        dgu_s[m, :, units:] = (d_up * r).astype(BF16)

    lead = jnp.minimum(1 + AHEAD * (last - place), micro)

    @pl.loop(0, micro + lead)
    def _(i):
        @pl.when((i == lead) & (place == 0))
        def _():
            turn_gate_up()

        @pl.when(i >= lead)
        def _():
            backward(i - lead)

        @pl.when((i == 0) & (place == 0) & (core == 1))
        def _():
            pl.semaphore_wait(turn, 1)

        @pl.when(i < micro)
        def _():
            forward(i)

        @pl.when((i == 0) & (place == 0) & (core == 0))
        def _():
            pl.semaphore_signal(turn, inc=1, device_id=sibling, device_id_type=MESH)

    rows = micro * x_in.shape[1]
    tile = width // depth
    own = tile // 4
    dgu_all = dgu_s[...].reshape(rows, 2 * units)
    hid_all = hid_s[...].reshape(rows, units)
    streams, stretch = ring_in.shape[0], ring_in.shape[-1]
    first_b = SIDE_FIRST
    middle = depth // 2

    def tile_at(j):
        turn_off = jnp.where(lax.rem(j, 2) == 1, middle - (j + 1) // 2, j // 2 + middle)
        return lax.rem(deep + jnp.where(j == depth - 1, 0, turn_off), depth)

    def weight_terms(j):
        q = tile_at(j)
        at = pl.multiple_of(q * tile, tile)
        xs = x_in[:, :, pl.ds(at, tile)].reshape(rows, tile)
        gs = g_in[:, :, pl.ds(at, tile)].reshape(rows, tile)
        for left, right, low in ((xs, dgu_all, 0), (gs, hid_all, 2 * units)):
            term = lax.dot_general(left, right, ROWS_ROWS, preferred_element_type=F32)
            high = low + right.shape[1]
            part[q, :, :, :, low:high] = term.astype(BF16).reshape(2, 2, own, high - low)
        for k in range(2):
            pltpu.make_async_remote_copy(
                part.at[q, k, 1 - core],
                from_core.at[q, k],
                core_send,
                core_recv.at[q],
                device_id=sibling,
                device_id_type=MESH,
            ).start()

    def terms(low, high):
        @pl.loop(low, high)
        def _(j):
            weight_terms(j)

    def columns(n):
        return slice(n * stretch, (n + 1) * stretch)

    def chip_sum(q, k, cols):
        return part[q, k, core, :, cols].astype(F32) + from_core[q, k, :, cols].astype(F32)

    side_cols = slice(0, first_b * stretch)

    def chip_ready(j):
        q = tile_at(j)
        pltpu.make_async_copy(from_core.at[q], from_core.at[q], core_recv.at[q]).wait()
        side_out[q] = chip_sum(q, 1 - side, side_cols).astype(BF16)
        pltpu.make_async_remote_copy(
            side_out.at[q],
            side_in.at[q],
            side_send,
            side_recv.at[q],
            device_id=partner,
            device_id_type=MESH,
        ).start()

    def side_ready(j):
        q = tile_at(j)
        pltpu.make_async_copy(side_in.at[q], side_in.at[q], side_recv.at[q]).wait()

    def own_sums(n, q):
        if n < first_b:
            return [(0, chip_sum(q, side, columns(n)) + side_in[q, :, columns(n)].astype(F32))]
        return [(k, chip_sum(q, k, columns(n))) for k in range(2)]

    def slot(ref, n, way, step):
        return ref.at[n, way, step, 0] if n < first_b else ref.at[n, way, step]

    def ring_wait(n, way, step):
        ref = slot(ring_in, n, way, step)
        pltpu.make_async_copy(ref, ref, ring_recv.at[n, way, step]).wait()

    def ring_step(step, group):
        for long in (False, True):
            for n in group:
                for way in range(2):
                    if (n % 2 == way) != long or (step == 0 and not long):
                        continue
                    q = lax.rem(deep + (middle - step if way == 0 else middle + step), depth)
                    held = step > (0 if long else 1)
                    if held:
                        ring_wait(n, way, step - 1)
                    for k, total in own_sums(n, q):
                        if held:
                            total = total + ring_in[n, way, step - 1, k].astype(F32)
                        ring_out[n, way, step, k] = total.astype(BF16)
                    pltpu.make_async_remote_copy(
                        slot(ring_out, n, way, step),
                        slot(ring_in, n, way, step),
                        ring_send.at[n, way],
                        ring_recv.at[n, way, step],
                        device_id=ring_to[way],
                        device_id_type=MESH,
                    ).start()

    def arrived(n, k):
        return ring_in[n, 0, middle - 1, k].astype(F32) + ring_in[n, 1, middle - 1, k].astype(F32)

    group_a, group_b = range(first_b), range(first_b, streams)
    terms(0, 2)
    chip_ready(0)
    ring_step(0, group_b)
    terms(2, 4)
    chip_ready(1)
    chip_ready(2)
    ring_step(1, group_b)
    terms(4, 6)
    chip_ready(3)
    chip_ready(4)
    side_ready(0)
    ring_step(0, group_a)
    ring_step(2, group_b)
    terms(6, 8)
    chip_ready(5)
    chip_ready(6)
    side_ready(1)
    side_ready(2)
    ring_step(1, group_a)
    ring_step(3, group_b)
    chip_ready(7)
    side_ready(3)
    side_ready(4)
    ring_step(2, group_a)
    for n in group_b:
        for way in range(2):
            ring_wait(n, way, middle - 1)
        end_out[n - first_b] = (
            chip_sum(deep, 1 - side, columns(n)) + arrived(n, 1 - side)
        ).astype(BF16)
        pltpu.make_async_remote_copy(
            end_out.at[n - first_b],
            end_in.at[n - first_b],
            end_send,
            end_recv.at[n - first_b],
            device_id=partner,
            device_id_type=MESH,
        ).start()
    side_ready(5)
    side_ready(6)
    ring_step(3, group_a)
    side_ready(7)
    whole = {}
    for n in group_b:
        ref = end_in.at[n - first_b]
        pltpu.make_async_copy(ref, ref, end_recv.at[n - first_b]).wait()
        whole[n] = (
            chip_sum(deep, side, columns(n))
            + arrived(n, side)
            + end_in[n - first_b].astype(F32)
        )
    for n in group_a:
        for way in range(2):
            ring_wait(n, way, middle - 1)
        whole[n] = own_sums(n, deep)[0][1] + arrived(n, 0)
    whole = jnp.concatenate([whole[n] for n in range(streams)], axis=1)
    grad_g[...] = whole[:, :units]
    grad_u[...] = whole[:, units : 2 * units]
    grad_d[...] = whole[:, 2 * units :]

    pltpu.make_async_copy(side_out, side_out, side_send).wait()
    pltpu.make_async_copy(end_out, end_out, end_send).wait()
    pltpu.make_async_copy(from_core, from_core, core_send).wait()
    for n in range(streams):
        for way in range(2):
            lowest = 0 if n % 2 == way else 1
            sent = ring_out.at[n, way, lowest:middle]
            if n < first_b:
                sent = ring_out.at[n, way, lowest:middle, 0]
            pltpu.make_async_copy(sent, sent, ring_send.at[n, way]).wait()

    @pl.when(place < last)
    def _():
        pltpu.make_async_copy(x_out, x_out, x_send).wait()

    @pl.when(place > 0)
    def _():
        pltpu.make_async_copy(g_out, g_out, g_send).wait()

    @pl.when(place == last)
    def _():
        pltpu.make_async_copy(g_in, g_in, c_send).wait()

    @pl.when(upper)
    def _():
        pltpu.make_async_copy(g_out, g_out, o_send).wait()

    pltpu.make_async_copy(g_out, grad_in, o_recv).wait()


def finish_kernel(wide_in, g_in, u_in, d_in, wide_out, g_out, u_out, d_out, wide, slim, into, out):
    size = wide.shape[0] // PIECES
    routes = [
        (wide_in.at[pl.ds(k * size, size)], wide.at[pl.ds(k * size, size)],
         wide_out.at[pl.ds(k * size, size)])
        for k in range(PIECES)
    ]
    for k, (src, dst) in enumerate(((g_in, g_out), (u_in, u_out), (d_in, d_out))):
        routes.append((src, slim.at[k], dst))
    for k, (src, held, _) in enumerate(routes):
        pltpu.make_async_copy(src, held, into.at[k]).start()
    for k, (src, held, dst) in enumerate(routes):
        pltpu.make_async_copy(src, held, into.at[k]).wait()
        pltpu.make_async_copy(held, dst, out.at[k]).start()
    for k, (_, held, dst) in enumerate(routes):
        pltpu.make_async_copy(held, dst, out.at[k]).wait()


def finished(wide, *slim):
    anywhere = pl.BlockSpec(memory_space=pl.ANY)
    arrays = (wide, *slim)
    return pl.pallas_call(
        finish_kernel,
        out_shape=tuple(jax.ShapeDtypeStruct(a.shape, a.dtype) for a in arrays),
        in_specs=[anywhere] * 4,
        out_specs=(anywhere,) * 4,
        scratch_shapes=[
            pltpu.VMEM(wide.shape, wide.dtype),
            pltpu.VMEM((3, *slim[0].shape), F32),
            pltpu.SemaphoreType.DMA((PIECES + 3,)),
            pltpu.SemaphoreType.DMA((PIECES + 3,)),
        ],
        compiler_params=pltpu.CompilerParams(vmem_limit_bytes=60 * 1024 * 1024),
        name="finish",
    )(*arrays)


def run_pipeline(tokens, cotangent, w_gate, w_up, w_down):
    sections = lax.axis_size("section")
    tok_rows, width = tokens.shape
    units = w_gate.shape[1]
    micro = MICRO
    rows = tok_rows // micro
    anywhere = pl.BlockSpec(memory_space=pl.ANY)
    wide = pltpu.VMEM((micro, rows, width), BF16)
    slim = pltpu.VMEM((micro, rows, units), BF16)
    slim_f = pltpu.VMEM((micro, rows, units), F32)
    weight = pltpu.VMEM((width, units), BF16)
    dma = pltpu.SemaphoreType.DMA
    grad = jax.ShapeDtypeStruct((width // lax.axis_size(DP), units), F32)
    streams, depth = STREAMS, lax.axis_size("dp_0")
    own, stretch = width // (4 * depth), 3 * units // streams
    vmem = pl.BlockSpec(memory_space=pltpu.VMEM)
    grad_in, *grads = pl.pallas_call(
        functools.partial(pipeline_kernel, sections, micro),
        out_shape=(
            jax.ShapeDtypeStruct((micro, rows, width), BF16),
            grad,
            grad,
            grad,
        ),
        in_specs=[anywhere] * 5,
        out_specs=(anywhere, vmem, vmem, vmem),
        scratch_shapes=[
            weight,
            weight,
            weight,
            pltpu.VMEM((units, width), BF16),
            pltpu.VMEM((2 * units, width), BF16),
            wide,
            wide,
            wide,
            wide,
            slim_f,
            slim_f,
            slim,
            pltpu.VMEM((micro, rows, 2 * units), BF16),
            pltpu.VMEM((micro, rows, 128), F32),
            pltpu.VMEM((depth, 2, 2, own, 3 * units), BF16),
            pltpu.VMEM((depth, 2, own, 3 * units), BF16),
            pltpu.VMEM((streams, 2, depth // 2, 2, own, stretch), BF16),
            pltpu.VMEM((streams, 2, depth // 2, 2, own, stretch), BF16),
            pltpu.VMEM((depth, own, SIDE_FIRST * stretch), BF16),
            pltpu.VMEM((depth, own, SIDE_FIRST * stretch), BF16),
            pltpu.VMEM((streams - SIDE_FIRST, own, stretch), BF16),
            pltpu.VMEM((streams - SIDE_FIRST, own, stretch), BF16),
            dma((3,)),
            pltpu.SemaphoreType.REGULAR,
            dma((micro,)),
            dma((micro,)),
            dma,
            dma,
            dma,
            dma,
            dma,
            dma,
            dma((depth,)),
            dma((streams, 2)),
            dma((streams, 2, depth // 2)),
            dma,
            dma((depth,)),
            dma,
            dma((streams - SIDE_FIRST,)),
        ],
        compiler_params=pltpu.CompilerParams(
            collective_id=0, has_side_effects=True, vmem_limit_bytes=56 * 1024 * 1024
        ),
        name="pipeline",
    )(
        tokens.reshape(micro, rows, width),
        cotangent.reshape(micro, rows, width),
        w_gate,
        w_up,
        w_down,
    )
    return finished(grad_in.reshape(tok_rows, width), *grads)


def body(tokens, cotangent, w_gate, w_up, w_down):
    outs = run_pipeline(tokens, cotangent, w_gate[0], w_up[0], w_down[0])
    return tuple(out[None] for out in outs)


def solution(mesh):
    torus = Mesh(
        mesh.devices.reshape(mesh.shape["section"], 8, 2, 2), ("section", "dp_0", "dp_1", "dp_2")
    )
    placed = (
        P(DP, None),
        P(DP, None),
        P("section", None, None),
        P("section", None, None),
        P("section", None, None),
    )
    return jax.shard_map(
        body,
        mesh=torus,
        in_specs=placed,
        out_specs=(
            P("section", DP, None),
            P("section", DP, None),
            P("section", DP, None),
            P("section", DP, None),
        ),
        check_vma=False,
    )
```

```python
import functools

import jax
import jax.numpy as jnp
from jax import lax
from jax.experimental import pallas as pl
from jax.experimental.pallas import tpu as pltpu
from jax.sharding import Mesh
from jax.sharding import PartitionSpec as P

MICRO = 15
AHEAD = 4
CHUNKS = 2
STREAMS = 6
SIDE_FIRST = 3
PIECES = 5
DP = ("dp_0", "dp_1", "dp_2")
MESH = pl.DeviceIdType.MESH
F32 = jnp.float32
BF16 = jnp.bfloat16
ROWS_ROWS = (((0,), (0,)), ((), ()))


def pipeline_kernel(
    sections,
    micro,
    tok,
    cot,
    wg_h,
    wu_h,
    wd_h,
    grad_in,
    grad_g,
    grad_u,
    grad_d,
    wg,
    wu,
    wd,
    wd_t,
    wgu_t,
    x_in,
    g_in,
    x_out,
    g_out,
    gate_s,
    up_s,
    hid_s,
    dgu_s,
    r_s,
    part,
    from_core,
    ring_in,
    ring_out,
    side_out,
    side_in,
    end_out,
    end_in,
    w_sem,
    turn,
    x_recv,
    g_recv,
    x_send,
    g_send,
    c_send,
    o_send,
    o_recv,
    core_send,
    core_recv,
    ring_send,
    ring_recv,
    side_send,
    side_recv,
    end_send,
    end_recv,
):
    place = lax.axis_index("section")
    deep = lax.axis_index("dp_0")
    side = lax.axis_index("dp_1")
    core = lax.axis_index("dp_2")
    depth = part.shape[0]
    half = sections // 2
    last = sections - 1
    upper = place >= half
    width = x_in.shape[2]
    units = wg.shape[1]
    span = width // CHUNKS
    chunks = [slice(k * span, (k + 1) * span) for k in range(CHUNKS)]

    weights = [
        pltpu.make_async_copy(src, dst, w_sem.at[k])
        for k, (src, dst) in enumerate(((wd_h, wd), (wg_h, wg), (wu_h, wu)))
    ]
    for copy in weights:
        copy.start()

    @pl.when(place == 0)
    def _():
        @pl.loop(0, micro)
        def _(m):
            pltpu.make_async_copy(tok.at[m], x_in.at[m], x_recv.at[m]).start()

    next_side = jnp.where(place == half - 1, 1 - side, side)
    prev_side = jnp.where(place == half, 1 - side, side)
    after = {"section": lax.rem(place + 1, sections), "dp_1": next_side}
    before = {"section": lax.rem(place + sections - 1, sections), "dp_1": prev_side}
    partner = {"dp_1": 1 - side}
    sibling = {"dp_2": 1 - core}
    ring_to = ({"dp_0": lax.rem(deep + 1, depth)}, {"dp_0": lax.rem(deep + depth - 1, depth)})

    barrier = pltpu.get_barrier_semaphore()

    @pl.when(place < last)
    def _():
        pl.semaphore_signal(barrier, inc=1, device_id=after, device_id_type=MESH)

    @pl.when(place > 0)
    def _():
        pl.semaphore_signal(barrier, inc=1, device_id=before, device_id_type=MESH)

    for friend in (partner, sibling, *ring_to):
        pl.semaphore_signal(barrier, inc=1, device_id=friend, device_id_type=MESH)
    block = width // depth

    def turned(src, dst, base):
        @pl.loop(0, depth)
        def _(k):
            at = pl.multiple_of(k * block, block)
            dst[base : base + units, pl.ds(at, block)] = src[pl.ds(at, block), :].T

    def turn_gate_up():
        turned(wg, wgu_t, 0)
        turned(wu, wgu_t, units)

    weights[0].wait()
    turned(wd, wd_t, 0)
    expected = 4 + jnp.where(place < last, 1, 0) + jnp.where(place > 0, 1, 0)
    pl.semaphore_wait(barrier, expected)

    @pl.when(place == last)
    def _():
        @pl.loop(0, micro)
        def _(m):
            pltpu.make_async_remote_copy(
                cot.at[m], g_in.at[m], c_send, g_recv.at[m], device_id=partner, device_id_type=MESH
            ).start()

    weights[1].wait()
    weights[2].wait()

    @pl.when(place > 0)
    def _():
        turn_gate_up()

    def forward(m):
        pltpu.make_async_copy(x_in.at[m], x_in.at[m], x_recv.at[m]).wait()
        x = x_in[m]
        gate = jnp.dot(x, wg[...], preferred_element_type=F32)
        up = jnp.dot(x, wu[...], preferred_element_type=F32)
        xf = x.astype(F32)
        r = lax.rsqrt(jnp.mean(xf * xf, axis=-1, keepdims=True) + 1e-06)
        gate = gate * r
        up = up * r
        hidden = (gate * jax.nn.sigmoid(gate) * up).astype(BF16)
        gate_s[m] = gate
        up_s[m] = up
        hid_s[m] = hidden
        r_s[m] = jnp.broadcast_to(r, (r.shape[0], 128))

        @pl.when(place < last)
        def _():
            for k, cols in enumerate(chunks):
                branch = jnp.dot(hidden, wd_t[:, cols], preferred_element_type=F32)
                x_out[m, :, cols] = (x_in[m, :, cols].astype(F32) + branch).astype(BF16)
                pltpu.make_async_remote_copy(
                    x_out.at[m, :, cols],
                    x_in.at[m, :, cols],
                    x_send,
                    x_recv.at[m],
                    device_id=after,
                    device_id_type=MESH,
                ).start()

    def backward(m):
        pltpu.make_async_copy(g_in.at[m], g_in.at[m], g_recv.at[m]).wait()
        d_hidden = jnp.dot(g_in[m], wd[...], preferred_element_type=F32)
        gate = gate_s[m]
        up = up_s[m]
        r = r_s[m, :, 0:1]
        sig = jax.nn.sigmoid(gate)
        d_gate = d_hidden * up * sig * (1.0 + gate * (1.0 - sig))
        d_up = d_hidden * gate * sig
        dg = d_gate.astype(BF16)
        du = d_up.astype(BF16)
        inner = jnp.sum(
            dg.astype(F32) * gate + du.astype(F32) * up, axis=-1, keepdims=True
        ) * (1.0 / width)
        shrink = r * inner
        dgu = jnp.concatenate([dg, du], axis=1)
        dgu_s[m, :, :units] = (d_gate * r).astype(BF16)
        dgu_s[m, :, units:] = (d_up * r).astype(BF16)
        for k, cols in enumerate(chunks):
            normed_grad = jnp.dot(dgu, wgu_t[:, cols], preferred_element_type=F32)
            g_out[m, :, cols] = (
                g_in[m, :, cols].astype(F32)
                + r * (normed_grad - x_in[m, :, cols].astype(F32) * shrink)
            ).astype(BF16)

            @pl.when(place > 0)
            def _():
                pltpu.make_async_remote_copy(
                    g_out.at[m, :, cols],
                    g_in.at[m, :, cols],
                    g_send,
                    g_recv.at[m],
                    device_id=before,
                    device_id_type=MESH,
                ).start()

        @pl.when(upper)
        def _():
            pltpu.make_async_remote_copy(
                g_out.at[m],
                grad_in.at[m],
                o_send,
                o_recv,
                device_id=partner,
                device_id_type=MESH,
            ).start()

        @pl.when(jnp.logical_not(upper))
        def _():
            pltpu.make_async_copy(g_out.at[m], grad_in.at[m], o_recv).start()

    lead = jnp.minimum(1 + AHEAD * (last - place), micro)

    @pl.loop(0, micro + lead)
    def _(i):
        @pl.when((i == lead) & (place == 0))
        def _():
            turn_gate_up()

        @pl.when(i >= lead)
        def _():
            backward(i - lead)

        @pl.when((i == 0) & (place == 0) & (core == 1))
        def _():
            pl.semaphore_wait(turn, 1)

        @pl.when(i < micro)
        def _():
            forward(i)

        @pl.when((i == 0) & (place == 0) & (core == 0))
        def _():
            pl.semaphore_signal(turn, inc=1, device_id=sibling, device_id_type=MESH)

    rows = micro * x_in.shape[1]
    tile = width // depth
    own = tile // 4
    dgu_all = dgu_s[...].reshape(rows, 2 * units)
    hid_all = hid_s[...].reshape(rows, units)
    streams, stretch = ring_in.shape[0], ring_in.shape[-1]
    first_b = SIDE_FIRST
    middle = depth // 2

    def tile_at(j):
        turn_off = jnp.where(lax.rem(j, 2) == 1, middle - (j + 1) // 2, j // 2 + middle)
        return lax.rem(deep + jnp.where(j == depth - 1, 0, turn_off), depth)

    def weight_terms(j):
        q = tile_at(j)
        at = pl.multiple_of(q * tile, tile)
        xs = x_in[:, :, pl.ds(at, tile)].reshape(rows, tile)
        gs = g_in[:, :, pl.ds(at, tile)].reshape(rows, tile)
        for left, right, low in ((xs, dgu_all, 0), (gs, hid_all, 2 * units)):
            term = lax.dot_general(left, right, ROWS_ROWS, preferred_element_type=F32)
            high = low + right.shape[1]
            part[q, :, :, :, low:high] = term.astype(BF16).reshape(2, 2, own, high - low)
        for k in range(2):
            pltpu.make_async_remote_copy(
                part.at[q, k, 1 - core],
                from_core.at[q, k],
                core_send,
                core_recv.at[q],
                device_id=sibling,
                device_id_type=MESH,
            ).start()

    def terms(low, high):
        @pl.loop(low, high)
        def _(j):
            weight_terms(j)

    def columns(n):
        return slice(n * stretch, (n + 1) * stretch)

    def chip_sum(q, k, cols):
        return part[q, k, core, :, cols].astype(F32) + from_core[q, k, :, cols].astype(F32)

    side_cols = slice(0, first_b * stretch)

    def chip_ready(j):
        q = tile_at(j)
        pltpu.make_async_copy(from_core.at[q], from_core.at[q], core_recv.at[q]).wait()
        side_out[q] = chip_sum(q, 1 - side, side_cols).astype(BF16)
        pltpu.make_async_remote_copy(
            side_out.at[q],
            side_in.at[q],
            side_send,
            side_recv.at[q],
            device_id=partner,
            device_id_type=MESH,
        ).start()

    def side_ready(j):
        q = tile_at(j)
        pltpu.make_async_copy(side_in.at[q], side_in.at[q], side_recv.at[q]).wait()

    def own_sums(n, q):
        if n < first_b:
            return [(0, chip_sum(q, side, columns(n)) + side_in[q, :, columns(n)].astype(F32))]
        return [(k, chip_sum(q, k, columns(n))) for k in range(2)]

    def slot(ref, n, way, step):
        return ref.at[n, way, step, 0] if n < first_b else ref.at[n, way, step]

    def ring_wait(n, way, step):
        ref = slot(ring_in, n, way, step)
        pltpu.make_async_copy(ref, ref, ring_recv.at[n, way, step]).wait()

    def ring_step(step, group):
        for long in (False, True):
            for n in group:
                for way in range(2):
                    if (n % 2 == way) != long or (step == 0 and not long):
                        continue
                    q = lax.rem(deep + (middle - step if way == 0 else middle + step), depth)
                    held = step > (0 if long else 1)
                    if held:
                        ring_wait(n, way, step - 1)
                    for k, total in own_sums(n, q):
                        if held:
                            total = total + ring_in[n, way, step - 1, k].astype(F32)
                        ring_out[n, way, step, k] = total.astype(BF16)
                    pltpu.make_async_remote_copy(
                        slot(ring_out, n, way, step),
                        slot(ring_in, n, way, step),
                        ring_send.at[n, way],
                        ring_recv.at[n, way, step],
                        device_id=ring_to[way],
                        device_id_type=MESH,
                    ).start()

    def arrived(n, k):
        return ring_in[n, 0, middle - 1, k].astype(F32) + ring_in[n, 1, middle - 1, k].astype(F32)

    group_a, group_b = range(first_b), range(first_b, streams)
    terms(0, 2)
    chip_ready(0)
    ring_step(0, group_b)
    terms(2, 4)
    chip_ready(1)
    chip_ready(2)
    ring_step(1, group_b)
    terms(4, 6)
    chip_ready(3)
    chip_ready(4)
    side_ready(0)
    ring_step(0, group_a)
    ring_step(2, group_b)
    terms(6, 8)
    chip_ready(5)
    chip_ready(6)
    side_ready(1)
    side_ready(2)
    ring_step(1, group_a)
    ring_step(3, group_b)
    chip_ready(7)
    side_ready(3)
    side_ready(4)
    ring_step(2, group_a)
    for n in group_b:
        for way in range(2):
            ring_wait(n, way, middle - 1)
        end_out[n - first_b] = (
            chip_sum(deep, 1 - side, columns(n)) + arrived(n, 1 - side)
        ).astype(BF16)
        pltpu.make_async_remote_copy(
            end_out.at[n - first_b],
            end_in.at[n - first_b],
            end_send,
            end_recv.at[n - first_b],
            device_id=partner,
            device_id_type=MESH,
        ).start()
    side_ready(5)
    side_ready(6)
    ring_step(3, group_a)
    side_ready(7)
    whole = {}
    for n in group_b:
        ref = end_in.at[n - first_b]
        pltpu.make_async_copy(ref, ref, end_recv.at[n - first_b]).wait()
        whole[n] = (
            chip_sum(deep, side, columns(n))
            + arrived(n, side)
            + end_in[n - first_b].astype(F32)
        )
    for n in group_a:
        for way in range(2):
            ring_wait(n, way, middle - 1)
        whole[n] = own_sums(n, deep)[0][1] + arrived(n, 0)
    whole = jnp.concatenate([whole[n] for n in range(streams)], axis=1)
    grad_g[...] = whole[:, :units]
    grad_u[...] = whole[:, units : 2 * units]
    grad_d[...] = whole[:, 2 * units :]

    pltpu.make_async_copy(side_out, side_out, side_send).wait()
    pltpu.make_async_copy(end_out, end_out, end_send).wait()
    pltpu.make_async_copy(from_core, from_core, core_send).wait()
    for n in range(streams):
        for way in range(2):
            lowest = 0 if n % 2 == way else 1
            sent = ring_out.at[n, way, lowest:middle]
            if n < first_b:
                sent = ring_out.at[n, way, lowest:middle, 0]
            pltpu.make_async_copy(sent, sent, ring_send.at[n, way]).wait()

    @pl.when(place < last)
    def _():
        pltpu.make_async_copy(x_out, x_out, x_send).wait()

    @pl.when(place > 0)
    def _():
        pltpu.make_async_copy(g_out, g_out, g_send).wait()

    @pl.when(place == last)
    def _():
        pltpu.make_async_copy(g_in, g_in, c_send).wait()

    @pl.when(upper)
    def _():
        pltpu.make_async_copy(g_out, g_out, o_send).wait()

    pltpu.make_async_copy(g_out, grad_in, o_recv).wait()


def finish_kernel(wide_in, g_in, u_in, d_in, wide_out, g_out, u_out, d_out, wide, slim, into, out):
    size = wide.shape[0] // PIECES
    routes = [
        (wide_in.at[pl.ds(k * size, size)], wide.at[pl.ds(k * size, size)],
         wide_out.at[pl.ds(k * size, size)])
        for k in range(PIECES)
    ]
    for k, (src, dst) in enumerate(((g_in, g_out), (u_in, u_out), (d_in, d_out))):
        routes.append((src, slim.at[k], dst))
    for k, (src, held, _) in enumerate(routes):
        pltpu.make_async_copy(src, held, into.at[k]).start()
    for k, (src, held, dst) in enumerate(routes):
        pltpu.make_async_copy(src, held, into.at[k]).wait()
        pltpu.make_async_copy(held, dst, out.at[k]).start()
    for k, (_, held, dst) in enumerate(routes):
        pltpu.make_async_copy(held, dst, out.at[k]).wait()


def finished(wide, *slim):
    anywhere = pl.BlockSpec(memory_space=pl.ANY)
    arrays = (wide, *slim)
    return pl.pallas_call(
        finish_kernel,
        out_shape=tuple(jax.ShapeDtypeStruct(a.shape, a.dtype) for a in arrays),
        in_specs=[anywhere] * 4,
        out_specs=(anywhere,) * 4,
        scratch_shapes=[
            pltpu.VMEM(wide.shape, wide.dtype),
            pltpu.VMEM((3, *slim[0].shape), F32),
            pltpu.SemaphoreType.DMA((PIECES + 3,)),
            pltpu.SemaphoreType.DMA((PIECES + 3,)),
        ],
        compiler_params=pltpu.CompilerParams(vmem_limit_bytes=60 * 1024 * 1024),
        name="finish",
    )(*arrays)


def run_pipeline(tokens, cotangent, w_gate, w_up, w_down):
    sections = lax.axis_size("section")
    tok_rows, width = tokens.shape
    units = w_gate.shape[1]
    micro = MICRO
    rows = tok_rows // micro
    anywhere = pl.BlockSpec(memory_space=pl.ANY)
    wide = pltpu.VMEM((micro, rows, width), BF16)
    slim = pltpu.VMEM((micro, rows, units), BF16)
    slim_f = pltpu.VMEM((micro, rows, units), F32)
    weight = pltpu.VMEM((width, units), BF16)
    dma = pltpu.SemaphoreType.DMA
    grad = jax.ShapeDtypeStruct((width // lax.axis_size(DP), units), F32)
    streams, depth = STREAMS, lax.axis_size("dp_0")
    own, stretch = width // (4 * depth), 3 * units // streams
    vmem = pl.BlockSpec(memory_space=pltpu.VMEM)
    grad_in, *grads = pl.pallas_call(
        functools.partial(pipeline_kernel, sections, micro),
        out_shape=(
            jax.ShapeDtypeStruct((micro, rows, width), BF16),
            grad,
            grad,
            grad,
        ),
        in_specs=[anywhere] * 5,
        out_specs=(anywhere, vmem, vmem, vmem),
        scratch_shapes=[
            weight,
            weight,
            weight,
            pltpu.VMEM((units, width), BF16),
            pltpu.VMEM((2 * units, width), BF16),
            wide,
            wide,
            wide,
            wide,
            slim_f,
            slim_f,
            slim,
            pltpu.VMEM((micro, rows, 2 * units), BF16),
            pltpu.VMEM((micro, rows, 128), F32),
            pltpu.VMEM((depth, 2, 2, own, 3 * units), BF16),
            pltpu.VMEM((depth, 2, own, 3 * units), BF16),
            pltpu.VMEM((streams, 2, depth // 2, 2, own, stretch), BF16),
            pltpu.VMEM((streams, 2, depth // 2, 2, own, stretch), BF16),
            pltpu.VMEM((depth, own, SIDE_FIRST * stretch), BF16),
            pltpu.VMEM((depth, own, SIDE_FIRST * stretch), BF16),
            pltpu.VMEM((streams - SIDE_FIRST, own, stretch), BF16),
            pltpu.VMEM((streams - SIDE_FIRST, own, stretch), BF16),
            dma((3,)),
            pltpu.SemaphoreType.REGULAR,
            dma((micro,)),
            dma((micro,)),
            dma,
            dma,
            dma,
            dma,
            dma,
            dma,
            dma((depth,)),
            dma((streams, 2)),
            dma((streams, 2, depth // 2)),
            dma,
            dma((depth,)),
            dma,
            dma((streams - SIDE_FIRST,)),
        ],
        compiler_params=pltpu.CompilerParams(
            collective_id=0, has_side_effects=True, vmem_limit_bytes=56 * 1024 * 1024
        ),
        name="pipeline",
    )(
        tokens.reshape(micro, rows, width),
        cotangent.reshape(micro, rows, width),
        w_gate,
        w_up,
        w_down,
    )
    return finished(grad_in.reshape(tok_rows, width), *grads)


def body(tokens, cotangent, w_gate, w_up, w_down):
    outs = run_pipeline(tokens, cotangent, w_gate[0], w_up[0], w_down[0])
    return tuple(out[None] for out in outs)


def solution(mesh):
    torus = Mesh(
        mesh.devices.reshape(mesh.shape["section"], 8, 2, 2), ("section", "dp_0", "dp_1", "dp_2")
    )
    placed = (
        P(DP, None),
        P(DP, None),
        P("section", None, None),
        P("section", None, None),
        P("section", None, None),
    )
    return jax.shard_map(
        body,
        mesh=torus,
        in_specs=placed,
        out_specs=(
            P("section", DP, None),
            P("section", DP, None),
            P("section", DP, None),
            P("section", DP, None),
        ),
        check_vma=False,
    )
```
